32 devices in a mesh: win: 8 (over z, y), seq: 4 (over x, core).
Axes of the slice: x: 2, y: 2, z: 4, core: 2. Of those that a mesh axis runs over, the one named last changes fastest.
Arguments:
- inputs: bfloat16 [8, 1024, 1536], P('win', 'seq'), may hold values from -6 to 6
- skips: bfloat16 [8, 2048, 1280], P('win', 'seq'), may hold values from -6 to 6
- counts: int32 [8, 2048, 2608], P('win', 'seq'), may hold values from 0 to 4, as said below
- ln1_gain: bfloat16 [1536], P(('win', 'seq')), may hold values from 0.5 to 1.5
- ln1_bias: bfloat16 [1536], P(('win', 'seq')), may hold values from -1 to 1
- w_query: bfloat16 [1536, 512], P(('win', 'seq')), may hold values from -0.15625 to 0.15625
- w_key: bfloat16 [1536, 512], P(('win', 'seq')), may hold values from -0.15625 to 0.15625
- w_value: bfloat16 [1536, 1536], P(('win', 'seq')), may hold values from -0.15625 to 0.15625
- w_rel: bfloat16 [32, 512], P(None, ('win', 'seq')), may hold values from -1 to 1
- content_bias: bfloat16 [512], P(('win', 'seq')), may hold values from -3 to 3
- position_bias: bfloat16 [512], P(('win', 'seq')), may hold values from -3 to 3
- w_out: bfloat16 [1536, 1536], P(('win', 'seq')), may hold values from -1.25 to 1.25
- ln2_gain: bfloat16 [1536], P(('win', 'seq')), may hold values from 0.5 to 1.5
- ln2_bias: bfloat16 [1536], P(('win', 'seq')), may hold values from -1 to 1
- w_in: bfloat16 [1536, 3072], P(('win', 'seq')), may hold values from -0.15625 to 0.15625
- b_in: bfloat16 [3072], P(('win', 'seq')), may hold values from -3 to 3
- w_hid: bfloat16 [3072, 1536], P(('win', 'seq')), may hold values from -0.109375 to 0.109375
- b_hid: bfloat16 [1536], P(('win', 'seq')), may hold values from -3 to 3
- w_up: bfloat16 [1536, 1536], P(('win', 'seq')), may hold values from -0.15625 to 0.15625
- w_skip: bfloat16 [1280, 1536], P(('win', 'seq')), may hold values from -0.15625 to 0.15625
- m_bias: bfloat16 [1536], P(('win', 'seq')), may hold values from -3 to 3
- w_depth: bfloat16 [3, 1536], P(None, ('win', 'seq')), may hold values from -2 to 2
- w_point: bfloat16 [1536, 1536], P(('win', 'seq')), may hold values from -0.15625 to 0.15625
- p_bias: bfloat16 [1536], P(('win', 'seq')), may hold values from -3 to 3
- w_head: bfloat16 [1536, 2608], P(('win', 'seq')), may hold values from -0.009765625 to 0.009765625
- head_bias: bfloat16 [2608], replicated, may hold values from 0.5 to 1.5
Outputs:
- loss: float32 [], replicated
- activations: bfloat16 [8, 2048, 1536], P('win', 'seq')
- grad_inputs: float32 [8, 1024, 1536], P('win', 'seq')
- grad_skips: float32 [8, 2048, 1280], P('win', 'seq')
- grad_ln1_gain: float32 [1536], P(('win', 'seq'))
- grad_ln1_bias: float32 [1536], P(('win', 'seq'))
- grad_w_query: float32 [1536, 512], P(('win', 'seq'))
- grad_w_key: float32 [1536, 512], P(('win', 'seq'))
- grad_w_value: float32 [1536, 1536], P(('win', 'seq'))
- grad_w_rel: float32 [32, 512], P(None, ('win', 'seq'))
- grad_content_bias: float32 [512], P(('win', 'seq'))
- grad_position_bias: float32 [512], P(('win', 'seq'))
- grad_w_out: float32 [1536, 1536], P(('win', 'seq'))
- grad_ln2_gain: float32 [1536], P(('win', 'seq'))
- grad_ln2_bias: float32 [1536], P(('win', 'seq'))
- grad_w_in: float32 [1536, 3072], P(('win', 'seq'))
- grad_b_in: float32 [3072], P(('win', 'seq'))
- grad_w_hid: float32 [3072, 1536], P(('win', 'seq'))
- grad_b_hid: float32 [1536], P(('win', 'seq'))
- grad_w_up: float32 [1536, 1536], P(('win', 'seq'))
- grad_w_skip: float32 [1280, 1536], P(('win', 'seq'))
- grad_m_bias: float32 [1536], P(('win', 'seq'))
- grad_w_depth: float32 [3, 1536], P(None, ('win', 'seq'))
- grad_w_point: float32 [1536, 1536], P(('win', 'seq'))
- grad_p_bias: float32 [1536], P(('win', 'seq'))
- grad_w_head: float32 [1536, 2608], P(('win', 'seq'))
- grad_head_bias: float32 [2608], replicated
The draws below stay inside these ranges and needn't reach their ends.
Inputs may be any that keep to these rules, and one draw needn't show every extreme that they name: counts are whole numbers from 0 to 4 (at bin p of a window at most 1 + 4p // 2048).
All inputs are finite; a program needn't handle non-finite values.
Results may differ from the reference program's by a relative error of at most 0.025.
Values may be sent and summed in bfloat16 or wider, within the bound.
No kernel may reach another device: no remote copies, remote signals or barrier semaphores. Data moves between devices by JAX's collectives and lax.ppermute only.
A program may use at most 384 MiB of HBM per device.

```python
import math
import jax
import jax.numpy as jnp
from jax import lax

D = 1536
HEADS = 8
KEY = 64
VAL = 192
FF = 3072
BASIS = 32
CS = 1280
TRACKS = 2608
HK = 512
HV = 1536
SEQ_LEN = 1024
BINS = 2048
WINS = 8


def draw_counts(key, part):
    position = jnp.arange(BINS, dtype=jnp.int32)
    upper_bound = 2 + 4 * position // BINS
    return jax.random.randint(key, (WINS, BINS, TRACKS), 0, upper_bound[None, :, None], dtype=jnp.int32)


def steps_of(own_key, dims, pieces, smallest, largest):
    loudness, own = 1.0, jax.random.fold_in(own_key, 6)
    for axis_at, parts in pieces:
        heights = jnp.exp(jax.random.uniform(jax.random.fold_in(own, axis_at), (parts,), jnp.float32, smallest / len(pieces), largest / len(pieces)))
        loudness = loudness * jnp.repeat(heights, dims[axis_at] // parts).reshape([-1 if axis == axis_at else 1 for axis in range(len(dims))])
    return loudness


def noise(key, extent, scale, bound, shards=(), kind=jnp.bfloat16):
    drawn = scale * jax.random.normal(key, extent, jnp.float32)
    if shards:
        drawn = drawn * steps_of(key, extent, shards, -0.22, 0.18)
    return jnp.clip(drawn, -bound, bound).astype(kind)


def setup_inputs(seed: int = 0) -> dict:
    seeds = jax.random.split(jax.random.key(seed), 27)
    return {
        "inputs": noise(seeds[0], (WINS, SEQ_LEN, D), 1.0, 6.0, ((0, 8), (1, 4))),
        "skips": noise(seeds[1], (WINS, BINS, CS), 1.0, 6.0, ((0, 8), (1, 4))),
        "counts": draw_counts(jax.random.fold_in(seeds[26], 71), 0),
        "ln1_gain": jnp.clip(1.0 + 0.1 * jax.random.normal(seeds[3], (D,), jnp.float32), 0.5, 1.5).astype(jnp.bfloat16),
        "ln1_bias": noise(seeds[4], (D,), 0.2, 1.0, ((0, 32),)),
        "w_query": noise(seeds[5], (D, HK), D ** -0.5, 0.15625, ((0, 32),)),
        "w_key": noise(seeds[6], (D, HK), D ** -0.5, 0.15625, ((0, 32),)),
        "w_value": noise(seeds[7], (D, HV), D ** -0.5, 0.15625, ((0, 32),)),
        "w_rel": noise(seeds[8], (BASIS, HK), BASIS ** -0.5, 1.0, ((1, 32),)),
        "content_bias": noise(seeds[9], (HK,), 0.5, 3.0, ((0, 32),)),
        "position_bias": noise(seeds[10], (HK,), 0.5, 3.0, ((0, 32),)),
        "w_out": noise(seeds[11], (HV, D), (max(HV // 64, 1)) ** -0.5, 1.25, ((0, 32),)),
        "ln2_gain": jnp.clip(1.0 + 0.1 * jax.random.normal(seeds[12], (D,), jnp.float32), 0.5, 1.5).astype(jnp.bfloat16),
        "ln2_bias": noise(seeds[13], (D,), 0.2, 1.0, ((0, 32),)),
        "w_in": noise(seeds[14], (D, FF), D ** -0.5, 0.15625, ((0, 32),)),
        "b_in": noise(seeds[15], (FF,), 0.5, 3.0, ((0, 32),)),
        "w_hid": noise(seeds[16], (FF, D), FF ** -0.5, 0.109375, ((0, 32),)),
        "b_hid": noise(seeds[17], (D,), 0.5, 3.0, ((0, 32),)),
        "w_up": noise(seeds[18], (D, D), D ** -0.5, 0.15625, ((0, 32),)),
        "w_skip": noise(seeds[19], (CS, D), CS ** -0.5, 0.15625, ((0, 32),)),
        "m_bias": noise(seeds[20], (D,), 0.5, 3.0, ((0, 32),)),
        "w_depth": noise(seeds[21], (3, D), 0.5, 2.0, ((1, 32),)),
        "w_point": noise(seeds[22], (D, D), D ** -0.5, 0.15625, ((0, 32),)),
        "p_bias": noise(seeds[23], (D,), 0.5, 3.0, ((0, 32),)),
        "w_head": noise(seeds[24], (D, TRACKS), (256 * D) ** -0.5, 0.009765625, ((0, 32),)),
        "head_bias": jnp.clip(jax.random.uniform(seeds[25], (TRACKS,), jnp.float32, 0.5, 1.5), 0.5, 1.5).astype(jnp.bfloat16),
    }


@jax.custom_vjp
def low(v):
    return lax.optimization_barrier(v.astype(jnp.bfloat16)).astype(jnp.float32)

@jax.custom_vjp
def low_back(v):
    return v

def low_keep(v):
    return (low(v), None)

def low_pass(kept, grad):
    return (grad,)

def back_keep(v):
    return (v, None)

def back_low(kept, grad):
    return (low(grad),)
low.defvjp(low_keep, low_pass)
low_back.defvjp(back_keep, back_low)
EPS = 1e-05
HIGH = lax.Precision.HIGHEST

def basis_table(offsets, seq_len, basis_count):
    halves = basis_count // 2
    ramped = jnp.arange(halves, dtype=jnp.int32).astype(jnp.float32) / (halves - 1)
    half_life = 3.0 * jnp.exp(ramped * math.log(seq_len / 3.0))
    distance = jnp.abs(offsets)[..., None]
    decays = jnp.exp(-math.log(2.0) * distance / half_life)
    return jnp.concatenate([decays, jnp.sign(offsets)[..., None] * decays], axis=-1)

def layer_norm(values, gain_row, bias_row):
    centred = values - lax.optimization_barrier(jnp.mean(values, axis=-1, keepdims=True))
    spread = lax.optimization_barrier(jnp.mean(centred * centred, axis=-1, keepdims=True))
    return centred * lax.rsqrt(spread + EPS) * gain_row + bias_row

def mix_block(queries, pos_query, key_rows, values, first_row, seq_len):
    row_pos = first_row.astype(jnp.int32) + jnp.arange(queries.shape[0], dtype=jnp.int32)
    col_pos = jnp.arange(key_rows.shape[0], dtype=jnp.int32)
    offsets = (row_pos[:, None] - col_pos[None, :]).astype(jnp.float32)
    basis_grid = low(basis_table(offsets, seq_len, BASIS))
    scores = jnp.einsum('qhk,chk->hqc', queries, key_rows, precision=HIGH)
    scores = scores + jnp.einsum('qhb,qcb->hqc', pos_query, basis_grid, precision=HIGH)
    scores = low_back(scores)
    weights = low(jax.nn.softmax(scores, axis=-1))
    return jnp.einsum('hqc,chv->qhv', weights, values, precision=HIGH)

def window(inputs_w, skips_w, counts_w, params):
    ln1_gain, ln1_bias, w_query, w_key, w_value, w_rel, content_bias, position_bias, w_out, ln2_gain, ln2_bias, w_in, b_in, w_hid, b_hid, w_up, w_skip, m_bias, w_depth, w_point, p_bias, w_head, head_bias = params
    length = inputs_w.shape[0]
    normed = low(layer_norm(inputs_w, ln1_gain, ln1_bias))
    query_raw = low_back(jnp.dot(normed, w_query, precision=HIGH)) * 0.125
    queries = low(low_back(query_raw + content_bias)).reshape(length, HEADS, KEY)
    pos_in = (query_raw + position_bias).reshape(length, HEADS, KEY)
    pos_query = low(low_back(jnp.einsum('lhk,bhk->lhb', pos_in, w_rel.reshape(BASIS, HEADS, KEY), precision=HIGH)))
    key_rows = low(low_back(jnp.dot(normed, w_key, precision=HIGH))).reshape(length, HEADS, KEY)
    values = low(low_back(jnp.dot(normed, w_value, precision=HIGH))).reshape(length, HEADS, VAL)
    blk_len = 512 if length % 512 == 0 else length
    blk_count = length // blk_len

    def block_step(block_item):
        return mix_block(block_item[0], block_item[1], key_rows, values, block_item[2], length)
    starts = jnp.arange(blk_count, dtype=jnp.int32) * blk_len
    attended = lax.map(jax.checkpoint(block_step), (queries.reshape(blk_count, blk_len, HEADS, KEY), pos_query.reshape(blk_count, blk_len, HEADS, BASIS), starts))
    attended = low(low_back(attended.reshape(length, HEADS * VAL)))
    resid_one = low_back(inputs_w + jnp.dot(attended, w_out, precision=HIGH))
    normed_two = low(layer_norm(resid_one, ln2_gain, ln2_bias))
    pre_act = low_back(jnp.dot(normed_two, w_in, precision=HIGH) + b_in)
    hidden = low(low_back(jax.nn.gelu(pre_act, approximate=True)))
    resid_two = low(low_back(resid_one + jnp.dot(hidden, w_hid, precision=HIGH) + b_hid))
    lifted = low_back(jnp.dot(resid_two, w_up, precision=HIGH))
    merged = low_back(jnp.repeat(lifted, 2, axis=0) + jnp.dot(skips_w, w_skip, precision=HIGH) + m_bias)
    padded = jnp.pad(merged, ((1, 1), (0, 0)))
    depth_out = w_depth[0] * padded[:-2] + w_depth[1] * padded[1:-1] + w_depth[2] * padded[2:]
    depth_out = low(low_back(depth_out))
    output = merged + jnp.dot(depth_out, w_point, precision=HIGH) + p_bias
    head_in = low(low_back(output))
    logits = low_back(jnp.dot(head_in, w_head, precision=HIGH) + head_bias)
    rate_rows = jax.nn.softplus(logits)
    total_rate = lax.optimization_barrier(jnp.sum(rate_rows, axis=0))
    total_count = lax.optimization_barrier(jnp.sum(counts_w, axis=0))
    log_total = jnp.log(total_rate)
    window_loss = -jnp.sum(counts_w * jnp.log(rate_rows)) + jnp.sum(total_count * log_total) + 0.2 * jnp.sum(total_rate - total_count * log_total)
    return (window_loss, output)

def reference(inputs, skips, counts, ln1_gain, ln1_bias, w_query, w_key, w_value, w_rel, content_bias, position_bias, w_out, ln2_gain, ln2_bias, w_in, b_in, w_hid, b_hid, w_up, w_skip, m_bias, w_depth, w_point, p_bias, w_head, head_bias):
    params = tuple((weight.astype(jnp.float32) for weight in (ln1_gain, ln1_bias, w_query, w_key, w_value, w_rel, content_bias, position_bias, w_out, ln2_gain, ln2_bias, w_in, b_in, w_hid, b_hid, w_up, w_skip, m_bias, w_depth, w_point, p_bias, w_head, head_bias)))
    count_rows = counts.astype(jnp.float32)

    def total_loss(inputs_f, skips_f, params_f):

        def window_step(running, item_row):
            window_loss, output = window(item_row[0], item_row[1], item_row[2], params_f)
            return (running + window_loss, output)
        return lax.scan(jax.checkpoint(window_step), jnp.zeros((), jnp.float32), (inputs_f, skips_f, count_rows))
    loss_sum, pullback, outputs = jax.vjp(total_loss, inputs.astype(jnp.float32), skips.astype(jnp.float32), params, has_aux=True)
    grad_inputs, grad_skips, grads = pullback(jnp.ones((), jnp.float32))
    loss_mean = loss_sum / (WINS * BINS * TRACKS)
    return (loss_mean, outputs.astype(jnp.bfloat16), grad_inputs, grad_skips, grads[0], grads[1], grads[2], grads[3], grads[4], grads[5], grads[6], grads[7], grads[8], grads[9], grads[10], grads[11], grads[12], grads[13], grads[14], grads[15], grads[16], grads[17], grads[18], grads[19], grads[20], grads[21], grads[22])
```

```python
import functools
import math

import jax
import jax.numpy as jnp
from jax import lax
from jax.experimental import pallas as pl
from jax.experimental.pallas import tpu as pltpu
from jax.sharding import PartitionSpec as P

D = 1536
HEADS = 8
KEY = 64
VAL = 192
BASIS = 32
CS = 1280
TRACKS = 2608
TOK_SEQ = 256
SEQS_DEV = 1
HK = 512
HV = 1536


WIN, SEQ = "win", "seq"
BOTH = (WIN, SEQ)
EPS = 1e-05
HIGH = lax.Precision.HIGHEST


def with_halo(cells, sides, width):
    for axis, dim in sides:
        count = lax.axis_size(axis)
        ends = count - 1
        head = lax.slice_in_dim(cells, 0, width, axis=dim)
        tail = lax.slice_in_dim(cells, cells.shape[dim] - width, cells.shape[dim], axis=dim)
        cells = jnp.concatenate(
            [
                lax.ppermute(tail, axis, [(i, (i + 1) % count) for i in range(ends)]),
                cells,
                lax.ppermute(head, axis, [((i + 1) % count, i) for i in range(ends)]),
            ],
            axis=dim,
        )
    return cells


def basis_table(offsets, seq_len, basis_count):
    halves = basis_count // 2
    ramped = jnp.arange(halves, dtype=jnp.int32).astype(jnp.float32) / (halves - 1)
    half_life = 3.0 * jnp.exp(ramped * math.log(seq_len / 3.0))
    distance = jnp.abs(offsets)[..., None]
    decays = jnp.exp(-math.log(2.0) * distance / half_life)
    return jnp.concatenate([decays, jnp.sign(offsets)[..., None] * decays], axis=-1)


def layer_norm(values, gain_row, bias_row):
    centred = values - jnp.mean(values, axis=-1, keepdims=True)
    spread = jnp.mean(centred * centred, axis=-1, keepdims=True)
    return centred * lax.rsqrt(spread + EPS) * gain_row + bias_row


def smooth_act(values):
    return jax.nn.gelu(values, approximate=True)


def product(first_arg, second_arg):
    return jnp.dot(first_arg, second_arg, preferred_element_type=jnp.float32)


def weight_product(first_arg, second_arg):
    return lax.dot_general(
        first_arg, second_arg, (((0,), (0,)), ((), ())), preferred_element_type=jnp.float32
    )


def input_product(first_arg, second_arg):
    return lax.dot_general(
        first_arg, second_arg, (((1,), (1,)), ((), ())), preferred_element_type=jnp.float32
    )


def score_block(query_blk, pos_blk, key_blk, query_first, key_first, seq_len):
    row_pos = query_first + jnp.arange(query_blk.shape[1], dtype=jnp.int32)
    col_pos = key_first + jnp.arange(key_blk.shape[1], dtype=jnp.int32)
    offsets = (row_pos[:, None] - col_pos[None, :]).astype(jnp.float32)
    basis_grid = basis_table(offsets, seq_len, BASIS).astype(jnp.bfloat16)
    key_heads = key_blk.reshape(key_blk.shape[0], key_blk.shape[1], HEADS, KEY)
    content = jnp.einsum(
        "snhk,schk->shnc", query_blk, key_heads, preferred_element_type=jnp.float32
    )
    position = jnp.einsum("snhb,ncb->shnc", pos_blk, basis_grid, preferred_element_type=jnp.float32)
    return (content + position, basis_grid)


F32 = jnp.float32
LOW = jnp.bfloat16
ROWS = 256
FF = 3072
RANKS = 4
WINDOWS = 8


def wide_table(seq_len):
    offsets = (seq_len - 1 - jnp.arange(2 * seq_len, dtype=jnp.int32)).astype(F32)
    return basis_table(offsets, seq_len, BASIS).astype(LOW).T


def offset_window(table_ref, keys):
    start = keys - ROWS - pl.program_id(0) * ROWS
    return table_ref[:, pl.ds(pl.multiple_of(start, 128), keys + ROWS)]


def row_scores(query, key, pos_query, window):
    keys = key.shape[0]
    wide = product(pos_query, window)
    lined = pltpu.roll(wide, keys + 1, 1, stride=1, stride_axis=0)
    return input_product(query, key) + lined[:, :keys]


def head_columns(head):
    return (
        slice(head * KEY, (head + 1) * KEY),
        slice(head * VAL, (head + 1) * VAL),
        slice(head * BASIS, (head + 1) * BASIS),
    )


def mix_kernel(heads, q_ref, k_ref, v_ref, pos_ref, table_ref, out_ref, norm_ref):
    window = offset_window(table_ref, k_ref.shape[0])
    for head in range(heads):
        ks, vs, bs = head_columns(head)
        scores = row_scores(q_ref[:, ks], k_ref[:, ks], pos_ref[:, bs], window)
        top = jnp.max(scores, axis=1, keepdims=True)
        powers = jnp.exp(scores - top)
        total = jnp.sum(powers, axis=1, keepdims=True)
        weights = (powers * (1.0 / total)).astype(LOW)
        out_ref[:, vs] = product(weights, v_ref[:, vs]).astype(LOW)
        norm_ref[:, head : head + 1] = top + jnp.log(total)


def mix_grad_kernel(
    heads,
    q_ref,
    k_ref,
    v_ref,
    pos_ref,
    table_ref,
    norm_ref,
    ga_ref,
    dq_ref,
    dpos_ref,
    dk_ref,
    dv_ref,
    dk_sum,
    dv_sum,
):
    step = pl.program_id(0)
    keys = k_ref.shape[0]
    window = offset_window(table_ref, keys)
    down = lax.broadcasted_iota(jnp.int32, (ROWS, ROWS), 0)
    across = lax.broadcasted_iota(jnp.int32, (ROWS, ROWS), 1)
    flip = (down + across == ROWS - 1).astype(LOW)

    @pl.when(step == 0)
    def _():
        dk_sum[...] = jnp.zeros_like(dk_sum)
        dv_sum[...] = jnp.zeros_like(dv_sum)

    for head in range(heads):
        ks, vs, bs = head_columns(head)
        query, key, value, grad = q_ref[:, ks], k_ref[:, ks], v_ref[:, vs], ga_ref[:, vs]
        scores = row_scores(query, key, pos_ref[:, bs], window)
        probs = jnp.exp(scores - norm_ref[:, head : head + 1])
        dprob = input_product(grad, value)
        delta = jnp.sum(probs * dprob, axis=1, keepdims=True)
        dscore = (probs * (dprob - delta)).astype(LOW)
        dq_ref[:, ks] = product(dscore, key).astype(LOW)
        dk_sum[:, ks] += weight_product(dscore, query)
        dv_sum[:, vs] += weight_product(probs.astype(LOW), grad)
        wide = jnp.concatenate([product(flip, dscore), jnp.zeros((ROWS, ROWS), F32)], axis=1)
        lined = pltpu.roll(wide, 0, 1, stride=1, stride_axis=0).astype(LOW)
        turned = input_product(lined, window).astype(LOW)
        dpos_ref[:, bs] = product(flip, turned).astype(LOW)

    @pl.when(step == pl.num_programs(0) - 1)
    def _():
        dk_ref[...] = dk_sum[...].astype(LOW)
        dv_ref[...] = dv_sum[...].astype(LOW)


def row_spec(array):
    return pl.BlockSpec((ROWS, array.shape[1]), lambda i: (i, 0))


def whole_spec(array):
    return pl.BlockSpec(array.shape, lambda i: (0, 0))


def mix(query, key, value, pos_query, table):
    rows, keys = query.shape[0], key.shape[0]
    heads = key.shape[1] // KEY
    norm = jax.ShapeDtypeStruct((rows, heads), F32)
    out = jax.ShapeDtypeStruct((rows, value.shape[1]), LOW)
    return pl.pallas_call(
        functools.partial(mix_kernel, heads),
        grid=(rows // ROWS,),
        in_specs=[
            row_spec(query),
            whole_spec(key),
            whole_spec(value),
            row_spec(pos_query),
            whole_spec(table),
        ],
        out_specs=[row_spec(out), row_spec(norm)],
        out_shape=[out, norm],
        compiler_params=pltpu.CompilerParams(vmem_limit_bytes=40 * 2**20),
        cost_estimate=pl.CostEstimate(
            flops=40 * rows * keys * heads * (KEY + BASIS + VAL),
            transcendentals=rows * keys * heads,
            bytes_accessed=4 * 2**20,
        ),
    )(query, key, value, pos_query, table)


def mix_grad(query, key, value, pos_query, table, norm, grad):
    rows, keys = query.shape[0], key.shape[0]
    heads = key.shape[1] // KEY

    def like(array):
        return jax.ShapeDtypeStruct(array.shape, LOW)

    return pl.pallas_call(
        functools.partial(mix_grad_kernel, heads),
        grid=(rows // ROWS,),
        in_specs=[
            row_spec(query),
            whole_spec(key),
            whole_spec(value),
            row_spec(pos_query),
            whole_spec(table),
            row_spec(norm),
            row_spec(grad),
        ],
        out_specs=[row_spec(query), row_spec(pos_query), whole_spec(key), whole_spec(value)],
        out_shape=[like(query), like(pos_query), like(key), like(value)],
        scratch_shapes=[pltpu.VMEM(key.shape, F32), pltpu.VMEM(value.shape, F32)],
        compiler_params=pltpu.CompilerParams(vmem_limit_bytes=40 * 2**20),
        cost_estimate=pl.CostEstimate(
            flops=60 * rows * keys * heads * (KEY + BASIS + VAL),
            transcendentals=rows * keys * heads,
            bytes_accessed=6 * 2**20,
        ),
    )(query, key, value, pos_query, table, norm, grad)


def trade(block, axis, bits):
    count = lax.axis_size(axis)
    return lax.ppermute(block, axis, [(i, i ^ bits) for i in range(count)])


def in_order(pieces, index):
    pieces = list(pieces)
    bit = 1
    while bit < len(pieces):
        odd = (index & bit) != 0
        pieces = [jnp.where(odd, pieces[k ^ bit], pieces[k]) for k in range(len(pieces))]
        bit *= 2
    return pieces


def place_kernel(axis, shift, inner, columns, *refs):
    index = lax.axis_index(axis)
    index = index // shift if shift > 1 else index
    count = len(refs) - 1
    out_ref = refs[count]
    for k in range(count):
        to = (index % count) ^ k
        if columns:
            width = refs[k].shape[1]
            out_ref[:, pl.ds(pl.multiple_of(to * width, 128), width)] = refs[k][...]
        elif inner:
            for outer in range(inner):
                out_ref[outer, to] = refs[k][outer]
        else:
            out_ref[to] = refs[k][...]


def place(pieces, axis, shift=1, inner=0, columns=False):
    count, shape = len(pieces), pieces[0].shape
    if columns:
        shape = (shape[0], count * shape[1])
    elif inner:
        shape = (inner, count) + shape[1:]
    else:
        shape = (count,) + shape
    return pl.pallas_call(
        functools.partial(place_kernel, axis, shift, inner, columns),
        out_shape=jax.ShapeDtypeStruct(shape, pieces[0].dtype),
        compiler_params=pltpu.CompilerParams(vmem_limit_bytes=24 * 2**20),
        cost_estimate=pl.CostEstimate(
            flops=0,
            transcendentals=0,
            bytes_accessed=2 * count * pieces[0].size * pieces[0].dtype.itemsize,
        ),
    )(*pieces)


def pick(blocks, index):
    return lax.dynamic_index_in_dim(blocks, index, 0, keepdims=False)


tie = lax.optimization_barrier


class Flow:
    def __init__(self, stages):
        self.stages, self.result = stages, None
        self.pending = next(stages)

    def step(self, arrived):
        try:
            self.pending = self.stages.send(arrived)
        except StopIteration as last:
            self.pending, self.result = (), last.value


def advance(values, *flows):
    values, arrived = tie((values, [flow.pending for flow in flows]))
    for flow, rows in zip(flows, arrived):
        flow.step(rows)
    return values


def seq_all(rows):
    near, far = yield trade(rows, SEQ, 1), trade(rows, SEQ, 2)
    last = yield trade(far, SEQ, 1)
    return place([rows, near, far, last], SEQ).reshape(RANKS * rows.shape[0], rows.shape[1])


def seq_sum(partial, rank):
    blocks = partial.reshape(RANKS, ROWS, partial.shape[1])
    sent = jnp.stack([pick(blocks, rank ^ 1), pick(blocks, rank ^ 3)]).astype(LOW)
    got = yield trade(sent, SEQ, 1)
    last = yield trade((pick(blocks, rank ^ 2) + got[1].astype(F32)).astype(LOW), SEQ, 2)
    return pick(blocks, rank) + got[0].astype(F32) + last.astype(F32)


def seq_swap(blocks, rank):
    got = yield [trade(pick(blocks, rank ^ k), SEQ, k) for k in range(1, RANKS)]
    return [pick(blocks, rank)] + got


def deal_kernel(parts, whole_ref, dealt_ref):
    width = whole_ref.shape[1] // (RANKS * parts)
    for t in range(RANKS):
        for p in range(parts):
            first = (p * RANKS + t) * width
            dealt_ref[t, :, p * width : (p + 1) * width] = whole_ref[:, first : first + width]


def deal(array, parts):
    rows, columns = array.shape
    return pl.pallas_call(
        functools.partial(deal_kernel, parts),
        out_shape=jax.ShapeDtypeStruct((RANKS, rows, columns // RANKS), array.dtype),
    )(array)


def undeal_kernel(parts, *refs):
    rank = lax.axis_index(SEQ)
    width = refs[0].shape[1] // parts
    pieces = [ref[...].astype(F32) for ref in refs[:RANKS]]
    for bit in (1, 2):
        odd = (rank & bit) != 0
        pieces = [jnp.where(odd, pieces[k ^ bit], pieces[k]) for k in range(RANKS)]
    for t in range(RANKS):
        for p in range(parts):
            first = (p * RANKS + t) * width
            refs[RANKS][:, first : first + width] = pieces[t][:, p * width : (p + 1) * width]


def undeal(pieces, parts):
    rows, columns = pieces[0].shape
    return pl.pallas_call(
        functools.partial(undeal_kernel, parts),
        out_shape=jax.ShapeDtypeStruct((rows, columns * RANKS), F32),
    )(*pieces)


ROOM = 640
EXTRA = 8
SHORT = {}
for _name, _size in (
    ("gain1", 48),
    ("bias1", 48),
    ("gain2", 48),
    ("bias2", 48),
    ("b_in", 96),
    ("b_hid", 48),
    ("m", 48),
    ("p", 48),
    ("d0", 48),
    ("d1", 48),
    ("d2", 48),
    ("con", 16),
    ("pos", 16),
):
    _first = sum(_high - _low for _low, _high in SHORT.values())
    SHORT[_name] = (_first, _first + _size)
DEVICES = WINDOWS * RANKS
REL = HK // DEVICES


def pack_kernel(names, *refs):
    out_ref = refs[-1]
    out_ref[...] = jnp.zeros_like(out_ref)
    for name, ref in zip(names, refs):
        low, high = SHORT[name]
        out_ref[0:1, low:high] = ref[...]
    for b in range(BASIS):
        out_ref[1:2, b * REL : (b + 1) * REL] = refs[-2][b : b + 1, :]


def pack(rows, rel):
    return pl.pallas_call(
        functools.partial(pack_kernel, tuple(rows)),
        out_shape=jax.ShapeDtypeStruct((EXTRA, ROOM), F32),
    )(*(row.astype(F32)[None] for row in rows.values()), rel.astype(F32))


WIDE = ("gain1", "bias1", "gain2", "bias2", "b_hid", "m", "p", "d0", "d1", "d2")


def unpack_kernel(table_ref, wide_ref, in_ref, con_ref, pos_ref, rel_ref):
    rank = lax.axis_index(SEQ)
    for d in range(DEVICES):
        line = table_ref[d][0:1]
        for number, name in enumerate(WIDE):
            low, high = SHORT[name]
            wide_ref[number : number + 1, d * 48 : (d + 1) * 48] = line[:, low:high]
    low, high = SHORT["b_in"]
    for w in range(WINDOWS):
        in_ref[0:1, w * 96 : (w + 1) * 96] = table_ref[RANKS * w + rank][0:1, low:high]
    here = DEVICES // RANKS
    for j in range(here):
        block = table_ref[here * rank + j]
        columns = slice(j * REL, (j + 1) * REL)
        for ref, name in ((con_ref, "con"), (pos_ref, "pos")):
            low, high = SHORT[name]
            ref[0:1, columns] = block[0:1, low:high]
        for b in range(BASIS):
            rel_ref[b : b + 1, columns] = block[1:2, b * REL : (b + 1) * REL]


def unpack(table):
    hq = HK // RANKS
    shapes = ((16, D), (1, FF // RANKS), (1, hq), (1, hq), (BASIS, hq))
    return pl.pallas_call(
        unpack_kernel, out_shape=[jax.ShapeDtypeStruct(shape, F32) for shape in shapes]
    )(table)


def pack_grads_kernel(names, *refs):
    rank = lax.axis_index(SEQ)
    wide, (in_ref, con_ref, pos_ref, rel_ref, out_ref) = refs[:-5], refs[-5:]
    out_ref[...] = jnp.zeros_like(out_ref)
    for d in range(DEVICES):
        for name, ref in zip(names, wide):
            low, high = SHORT[name]
            out_ref[d, 0:1, low:high] = ref[0:1, d * 48 : (d + 1) * 48]
    low, high = SHORT["b_in"]
    for w in range(WINDOWS):
        out_ref[RANKS * w + rank, 0:1, low:high] = in_ref[0:1, w * 96 : (w + 1) * 96]
    here = DEVICES // RANKS
    for j in range(here):
        columns = slice(j * REL, (j + 1) * REL)
        for ref, name in ((con_ref, "con"), (pos_ref, "pos")):
            low, high = SHORT[name]
            out_ref[here * rank + j, 0:1, low:high] = ref[0:1, columns]
        for b in range(BASIS):
            out_ref[here * rank + j, 1:2, b * REL : (b + 1) * REL] = rel_ref[
                b : b + 1, columns
            ]


def pack_grads(rows, in_row, con, pos, rel):
    return pl.pallas_call(
        functools.partial(pack_grads_kernel, tuple(rows)),
        out_shape=jax.ShapeDtypeStruct((DEVICES, EXTRA, ROOM), F32),
    )(*(row.reshape(1, -1) for row in rows.values()), in_row[None], con[None], pos[None], rel)


def finish_kernel(hq, hv, height, *refs):
    rank = lax.axis_index(SEQ)
    pieces, (q_ref, k_ref, v_ref, short_ref, rel_ref) = refs[:RANKS], refs[RANKS:]
    extra = jnp.zeros((EXTRA, ROOM), F32)
    for k in range(RANKS):
        block = pieces[k][...].astype(F32)
        t = rank ^ k
        weights = block[:height]
        narrow = pl.ds(pl.multiple_of(t * hq, 128), hq)
        q_ref[:, narrow] = weights[:, :hq]
        k_ref[:, narrow] = weights[:, hq : 2 * hq]
        v_ref[:, pl.ds(pl.multiple_of(t * hv, 128), hv)] = weights[:, 2 * hq :]
        extra = extra + block[height:]
    short_ref[...] = extra[0:1]
    for b in range(BASIS):
        rel_ref[b : b + 1, :] = extra[1:2, b * REL : (b + 1) * REL]


def finish(pieces, hq, hv):
    height = pieces[0].shape[0] - EXTRA
    shapes = ((height, HK), (height, HK), (height, HV), (1, ROOM), (BASIS, REL))
    return pl.pallas_call(
        functools.partial(finish_kernel, hq, hv, height),
        out_shape=[jax.ShapeDtypeStruct(shape, F32) for shape in shapes],
    )(*pieces)


def edges(rows, axis):
    count = lax.axis_size(axis)
    below, above = yield (
        lax.ppermute(rows[-1:], axis, [(i, i + 1) for i in range(count - 1)]),
        lax.ppermute(rows[:1], axis, [(i + 1, i) for i in range(count - 1)]),
    )
    return jnp.concatenate([below, rows, above], axis=0)


def win_all(block):
    got = yield [trade(block, WIN, 2 * k) for k in range(1, WINDOWS // 2)]
    column = place([block] + got, WIN, 2)
    beside = yield trade(column, WIN, 1)
    both = place([column, beside], WIN, 1, WINDOWS // 2)
    return both.reshape((WINDOWS,) + block.shape)


def win_sum(parts, window):
    z, y = window // 2, window % 2
    parts = parts.reshape((WINDOWS // 2, 2) + parts.shape[1:])
    sent = lax.dynamic_index_in_dim(parts, 1 - y, 1, keepdims=False)
    kept = lax.dynamic_index_in_dim(parts, y, 1, keepdims=False)
    got = yield trade(sent, WIN, 1)
    column = (kept.astype(F32) + got.astype(F32)).astype(LOW)
    got = yield [trade(pick(column, z ^ k), WIN, 2 * k) for k in range(1, WINDOWS // 2)]
    total = pick(column, z).astype(F32)
    for piece in got:
        total = total + piece.astype(F32)
    return total


def shared_sum(row):
    for axis, bits in ((SEQ, 1), (SEQ, 2), (WIN, 1), (WIN, 2), (WIN, 4)):
        got = yield trade(row, axis, bits)
        row = row + got
    return row


def core_sum(first_arg, second_arg, rank):
    core = rank % 2
    half = second_arg.shape[1] // 2
    other = lax.dynamic_slice_in_dim(second_arg, (1 - core) * half, half, 1)
    mine = lax.dynamic_slice_in_dim(second_arg, core * half, half, 1)
    got = yield trade(weight_product(first_arg, other).astype(LOW), SEQ, 1)
    total = (weight_product(first_arg, mine) + got.astype(F32)).astype(LOW)
    return total.reshape(4, 2, 2, total.shape[0] // 16, half)


def chip_sum(grads, rank, window):
    z, y = window // 2, window % 2
    x, core = rank // 2, rank % 2

    def at(yy, xx):
        cut = [
            lax.dynamic_slice(g, (0, yy, xx, 0, 0), (4, 1, 1) + g.shape[3:]).reshape(
                (4,) + g.shape[3:]
            )
            for g in grads
        ]
        return cut[0] if len(cut) == 1 else jnp.concatenate(cut, axis=1)

    def plus(a, b):
        return (a.astype(F32) + b.astype(F32)).astype(LOW)

    corner = at(1 - y, 1 - x)
    by_x, by_y = yield trade(corner[:2], SEQ, 2), trade(corner[2:], WIN, 1)
    over_y, over_x = at(1 - y, x), at(y, 1 - x)
    over_y = jnp.concatenate([plus(over_y[:2], by_x), over_y[2:]])
    over_x = jnp.concatenate([over_x[:2], plus(over_x[2:], by_y)])
    from_y, from_x = yield trade(over_y, WIN, 1), trade(over_x, SEQ, 2)
    own = (at(y, x).astype(F32) + from_y.astype(F32) + from_x.astype(F32)).astype(LOW)
    got = yield [trade(pick(own, z ^ k), WIN, 2 * k) for k in range(1, 4)]
    total = pick(own, z).astype(F32)
    for piece in got:
        total = total + piece.astype(F32)
    parts, first = [], 0
    for g in grads:
        rows, half = g.shape[3] // 2, g.shape[4]
        block = total[first : first + 2 * rows].reshape(2, rows, half)
        first += 2 * rows
        parts.append((pick(block, core), pick(block, 1 - core)))
    got = yield trade(jnp.concatenate([sent for _, sent in parts], axis=0), SEQ, 1)
    results, first = [], 0
    for kept, sent in parts:
        piece = got[first : first + sent.shape[0]]
        first += sent.shape[0]
        results.append(jnp.concatenate(in_order([kept, piece], core), axis=1))
    return results


def split_body(
    inputs,
    skips,
    counts,
    ln1_gain,
    ln1_bias,
    w_query,
    w_key,
    w_value,
    w_rel,
    content_bias,
    position_bias,
    w_out,
    ln2_gain,
    ln2_bias,
    w_in,
    b_in,
    w_hid,
    b_hid,
    w_up,
    w_skip,
    m_bias,
    w_depth,
    w_point,
    p_bias,
    w_head,
    head_bias,
):
    window, rank = lax.axis_index(WIN), lax.axis_index(SEQ)
    seq_len = ROWS * RANKS
    hq, hv, ff = HK // RANKS, HV // RANKS, FF // RANKS

    packed = pack(
        {
            "gain1": ln1_gain,
            "bias1": ln1_bias,
            "gain2": ln2_gain,
            "bias2": ln2_bias,
            "b_in": b_in,
            "b_hid": b_hid,
            "m": m_bias,
            "p": p_bias,
            "d0": w_depth[0],
            "d1": w_depth[1],
            "d2": w_depth[2],
            "con": content_bias,
            "pos": position_bias,
        },
        w_rel,
    ).astype(LOW)
    qkv_local = jnp.stack(
        [
            jnp.concatenate(
                [
                    jnp.concatenate(
                        [
                            w_query[:, t * hq : (t + 1) * hq],
                            w_key[:, t * hq : (t + 1) * hq],
                            w_value[:, t * hv : (t + 1) * hv],
                        ],
                        axis=1,
                    ),
                    packed,
                ]
            )
            for t in range(RANKS)
        ]
    )
    inputs_own = inputs.reshape(ROWS, D)
    qkv_flow = Flow(seq_swap(qkv_local, rank))
    inputs_flow = Flow(seq_all(inputs_own))
    out_full = lax.all_gather(w_out, BOTH, axis=0, tiled=True)
    late_local = jnp.concatenate([w_up, w_skip, w_point])
    w_in, late_local = advance((w_in, late_local), qkv_flow)
    qkv_flow = Flow(win_all(place(qkv_flow.result, SEQ).reshape(-1, ROOM)))
    in_flow = Flow(seq_swap(deal(w_in, WINDOWS), rank))
    late_full = lax.all_gather(late_local, BOTH, axis=0)
    w_hid = advance(w_hid, qkv_flow, in_flow, inputs_flow)
    in_flow = Flow(win_all(place(in_flow.result, SEQ).reshape(-1, ff)))
    hid_flow = Flow(win_all(w_hid))
    w_head = advance(w_head, qkv_flow, inputs_flow)
    head_full = lax.all_gather(w_head, BOTH, axis=0, tiled=True)
    gathered = qkv_flow.result.reshape(DEVICES, -1, ROOM)
    height = gathered.shape[1] - EXTRA
    qkv_part = gathered[:, :height].reshape(D, ROOM)
    inputs_all = inputs_flow.result
    wide, in_bias, content, position, rel_part = unpack(gathered[:, height:].astype(F32))
    row_of = {name: wide[number] for number, name in enumerate(WIDE)}
    depth_full = [row_of[name] for name in ("d0", "d1", "d2")]
    r_up, r_skip = w_up.shape[0], w_skip.shape[0]
    up_full = late_full[:, :r_up].reshape(D, D)
    skip_full = late_full[:, r_up : r_up + r_skip].reshape(CS, D)
    point_full = late_full[:, r_up + r_skip :].reshape(D, D)
    heads_here = hq // KEY
    same_head = (
        jnp.arange(hq)[:, None] // KEY == jnp.arange(heads_here * BASIS)[None, :] // BASIS
    )
    rel_square = jnp.where(same_head, jnp.tile(rel_part.T, (1, heads_here)), 0.0)
    gain_one, bias_one = row_of["gain1"], row_of["bias1"]
    gain_two, bias_two = row_of["gain2"], row_of["bias2"]

    normed = layer_norm(inputs_all.astype(F32), gain_one, bias_one).astype(LOW)
    projected = product(normed, qkv_part)
    query_raw = projected[:, :hq] * 0.125
    queries = (query_raw + content).astype(LOW)
    pos_in = query_raw + position
    pos_query = jnp.dot(pos_in, rel_square, precision=HIGH).astype(LOW)
    keys = projected[:, hq : 2 * hq].astype(LOW)
    values = projected[:, 2 * hq :].astype(LOW)
    offsets = wide_table(seq_len)
    queries, keys, values, pos_query = advance(
        (queries, keys, values, pos_query), in_flow, hid_flow
    )
    mixed, norms = advance(mix(queries, keys, values, pos_query, offsets))
    swap = Flow(seq_swap(mixed.reshape(RANKS, ROWS, hv), rank))
    advance((), swap)
    attended = place(swap.result, SEQ, columns=True)
    inputs_f = inputs_own.astype(F32)
    resid_one = inputs_f + product(attended, out_full)
    normed_flow = Flow(seq_all(layer_norm(resid_one, gain_two, bias_two).astype(LOW)))
    advance((), normed_flow, in_flow, hid_flow)
    advance((), normed_flow)
    normed_two = normed_flow.result
    in_part = in_flow.result.reshape(D, ff)
    hid_part = hid_flow.result.reshape(ff, D)
    pre_act = product(normed_two, in_part) + in_bias
    hidden = smooth_act(pre_act).astype(LOW)
    ff_flow = Flow(seq_sum(product(hidden, hid_part), rank))
    skip_rows = advance(skips.reshape(2 * ROWS, CS), ff_flow)
    from_skips = product(skip_rows, skip_full) + row_of["m"]
    from_skips = advance(from_skips, ff_flow)
    lift_in = (resid_one + ff_flow.result + row_of["b_hid"]).astype(LOW)
    twice = (jnp.arange(2 * ROWS)[:, None] // 2 == jnp.arange(ROWS)[None, :]).astype(LOW)
    merged = product(product(twice, lift_in).astype(LOW), up_full) + from_skips
    merged_flow = Flow(edges(merged.astype(LOW), SEQ))
    merged = advance(merged, merged_flow)
    padded = merged_flow.result.astype(F32)
    depth_out = (
        depth_full[0] * padded[:-2] + depth_full[1] * padded[1:-1] + depth_full[2] * padded[2:]
    ).astype(LOW)
    output = merged + product(depth_out, point_full) + row_of["p"]
    head_rows = output.astype(LOW)
    logits = product(head_rows, head_full) + head_bias.astype(F32)
    rate_rows = jax.nn.softplus(logits)
    count_rows = counts.reshape(2 * ROWS, TRACKS).astype(F32)
    total_rate, total_count = lax.psum(
        (jnp.sum(rate_rows, axis=0), jnp.sum(count_rows, axis=0)), SEQ
    )
    log_total = jnp.log(total_rate)
    window_terms = jnp.sum(total_count * log_total) + 0.2 * jnp.sum(
        total_rate - total_count * log_total
    )
    local_loss = -jnp.sum(count_rows * jnp.log(rate_rows)) + jnp.where(
        rank == 0, window_terms, 0.0
    )
    grad_rate = -count_rows / rate_rows + (0.2 + 0.8 * (total_count / total_rate))
    grad_rows = (grad_rate * jax.nn.sigmoid(logits)).astype(LOW)
    head_bias_part = jnp.sum(grad_rows, axis=0, dtype=F32)
    shared_flow = Flow(shared_sum(jnp.concatenate([head_bias_part, local_loss[None]])))
    spare = -TRACKS % 256
    head_core = Flow(core_sum(head_rows, jnp.pad(grad_rows, ((0, 0), (0, spare))), rank))
    grad_out = input_product(grad_rows, head_full).astype(LOW)
    pbias_grad = jnp.sum(grad_out, axis=0, dtype=F32)
    grad_depth = input_product(grad_out, point_full).astype(LOW)
    grad_out, grad_depth, pbias_grad = advance((grad_out, grad_depth, pbias_grad), head_core)
    depth_flow = Flow(edges(grad_depth, SEQ))
    head_flow = Flow(chip_sum([head_core.result], rank, window))
    depth_grad = jnp.stack(
        [
            jnp.sum(grad_depth * padded[:-2], axis=0),
            jnp.sum(grad_depth * padded[1:-1], axis=0),
            jnp.sum(grad_depth * padded[2:], axis=0),
        ]
    )
    point_core = Flow(core_sum(depth_out, grad_out, rank))
    grad_out, depth_grad = advance((grad_out, depth_grad), depth_flow)
    depth_pad = depth_flow.result
    merged_low = (
        grad_out.astype(F32)
        + depth_full[0] * depth_pad[2:]
        + depth_full[1] * depth_pad[1:-1]
        + depth_full[2] * depth_pad[:-2]
    ).astype(LOW)
    mbias_grad = jnp.sum(merged_low, axis=0, dtype=F32)
    lift_grad = weight_product(twice, merged_low).astype(LOW)
    grad_two = input_product(lift_grad, up_full).astype(LOW)
    hbias_grad = jnp.sum(grad_two, axis=0, dtype=F32)
    grad_two, merged_low, lift_grad, mbias_grad, hbias_grad = advance(
        (grad_two, merged_low, lift_grad, mbias_grad, hbias_grad), head_flow, point_core
    )
    two_flow = Flow(seq_all(grad_two))
    skip_core = Flow(core_sum(skip_rows, merged_low, rank))
    up_core = Flow(core_sum(lift_in, lift_grad, rank))
    skip_grad = input_product(merged_low, skip_full).reshape(1, 2 * ROWS, CS)
    skip_grad = advance(skip_grad, skip_core, up_core)
    tail_flow = Flow(
        chip_sum([point_core.result, skip_core.result, up_core.result], rank, window)
    )
    advance((), two_flow, shared_flow)
    advance((), two_flow, shared_flow)
    grad_two_all = two_flow.result
    grad_hidden = input_product(grad_two_all, hid_part).astype(LOW)
    _, pull_act = jax.vjp(smooth_act, pre_act)
    grad_pre = pull_act(grad_hidden.astype(F32))[0].astype(LOW)
    ibias_part = jnp.sum(grad_pre, axis=0, dtype=F32)
    pre_flow = Flow(seq_sum(input_product(grad_pre, in_part), rank))
    hid_low = weight_product(hidden, grad_two_all).astype(LOW)
    hid_low, grad_pre, ibias_part = advance(
        (hid_low, grad_pre, ibias_part), pre_flow, head_flow, tail_flow, shared_flow
    )
    hid_flow = Flow(win_sum(hid_low.reshape(WINDOWS, ff // WINDOWS, D), window))
    in_low = weight_product(normed_two, grad_pre).astype(LOW)
    in_low = advance(in_low, pre_flow, shared_flow)
    in_flow = Flow(win_sum(in_low.reshape(WINDOWS, D // WINDOWS, ff), window))
    _, pull_two = jax.vjp(layer_norm, resid_one, gain_two, bias_two)
    grad_resid, gain_two_grad, bias_two_grad = pull_two(pre_flow.result)
    grad_one = (grad_two.astype(F32) + grad_resid).astype(LOW)
    grad_att = input_product(grad_one, out_full).astype(LOW)
    att_flow = Flow(
        seq_swap(
            jnp.stack([grad_att[:, t * hv : (t + 1) * hv] for t in range(RANKS)]), rank
        )
    )
    out_core = Flow(core_sum(attended, grad_one, rank))
    grad_one, gain_two_grad, bias_two_grad = advance(
        (grad_one, gain_two_grad, bias_two_grad),
        head_flow,
        tail_flow,
        hid_flow,
        out_core,
        shared_flow,
    )
    out_flow = Flow(chip_sum([out_core.result], rank, window))
    advance((), att_flow, head_flow)
    grad_att = place(att_flow.result, SEQ).reshape(seq_len, hv)
    query_low, pos_low, key_grad, value_grad = mix_grad(
        queries, keys, values, pos_query, offsets, norms, grad_att
    )
    query_low, pos_low, key_grad, value_grad = advance(
        (query_low, pos_low, key_grad, value_grad), in_flow, hid_flow, out_flow, tail_flow
    )
    pos_f = pos_low.astype(F32)
    pos_in_grad = lax.dot_general(
        pos_f, rel_square, (((1,), (1,)), ((), ())), precision=HIGH
    )
    query_grad = (0.125 * (query_low.astype(F32) + pos_in_grad)).astype(LOW)
    qkv_out = jnp.concatenate([query_grad, key_grad, value_grad], axis=1)
    content_part = jnp.sum(query_low, axis=0, dtype=F32)
    rel_cross = lax.dot_general(pos_f, pos_in, (((0,), (0,)), ((), ())), precision=HIGH)
    rel_rows = jnp.sum(
        jnp.where(same_head.T, rel_cross, 0.0).reshape(heads_here, BASIS, hq), axis=0
    )
    position_part = jnp.sum(pos_in_grad, axis=0)
    partial = input_product(qkv_out, qkv_part)
    centred = inputs_all.astype(F32)
    centred = centred - jnp.mean(centred, axis=-1, keepdims=True)
    scale = lax.rsqrt(jnp.mean(centred * centred, axis=-1, keepdims=True) + EPS)
    gain_one_grad = jnp.sum(partial * (centred * scale), axis=0)
    bias_one_grad = jnp.sum(partial, axis=0)
    one_flow = Flow(seq_sum(partial, rank))
    extra = pack_grads(
        {
            "gain1": gain_one_grad,
            "bias1": bias_one_grad,
            "gain2": gain_two_grad,
            "bias2": bias_two_grad,
            "b_hid": hbias_grad,
            "m": mbias_grad,
            "p": pbias_grad,
            "d0": depth_grad[0],
            "d1": depth_grad[1],
            "d2": depth_grad[2],
        },
        ibias_part,
        content_part,
        position_part,
        rel_rows,
    ).astype(LOW)
    qkv_low = weight_product(normed, qkv_out).astype(LOW).reshape(DEVICES, -1, ROOM)
    qkv_flow = Flow(
        win_sum(
            jnp.concatenate([qkv_low, extra], axis=1).reshape(WINDOWS, -1, ROOM), window
        )
    )
    advance((), one_flow, in_flow, out_flow, tail_flow)
    in_back = Flow(seq_swap(in_flow.result.astype(LOW).reshape(RANKS, -1, ff), rank))
    advance((), one_flow, qkv_flow)
    grad_normed = one_flow.result
    _, pull_one = jax.vjp(lambda rows: layer_norm(rows, gain_one, bias_one), inputs_f)
    (grad_norm_in,) = pull_one(grad_normed)
    grad_inputs = (grad_one.astype(F32) + grad_norm_in).reshape(1, ROWS, D)
    advance((), out_flow, in_back)
    advance((), qkv_flow, out_flow)
    qkv_flow = Flow(seq_swap(qkv_flow.result.astype(LOW).reshape(RANKS, -1, ROOM), rank))
    advance((), qkv_flow)
    wq_grad, wk_grad, wv_grad, shorts, rel_grad = finish(qkv_flow.result, hq, hv)
    sums = {name: shorts[0, low:high] for name, (low, high) in SHORT.items()}
    in_grad = undeal(in_back.result, WINDOWS)
    point_grad, skip_weight_grad, up_grad = tail_flow.result
    (out_grad,) = out_flow.result
    head_grad = head_flow.result[0][:, :TRACKS]
    hid_grad = hid_flow.result
    loss_total, head_bias_grad = shared_flow.result[-1], shared_flow.result[:-1]
    loss_mean = loss_total / (WINDOWS * 2 * seq_len * TRACKS)
    return (
        loss_mean,
        head_rows.reshape(1, 2 * ROWS, D),
        grad_inputs,
        skip_grad,
        sums["gain1"],
        sums["bias1"],
        wq_grad,
        wk_grad,
        wv_grad,
        rel_grad,
        sums["con"],
        sums["pos"],
        out_grad,
        sums["gain2"],
        sums["bias2"],
        in_grad,
        sums["b_in"],
        hid_grad,
        sums["b_hid"],
        up_grad,
        skip_weight_grad,
        sums["m"],
        jnp.stack([sums["d0"], sums["d1"], sums["d2"]]),
        point_grad,
        sums["p"],
        head_grad,
        head_bias_grad,
    )


def general_body(
    inputs,
    skips,
    counts,
    ln1_gain,
    ln1_bias,
    w_query,
    w_key,
    w_value,
    w_rel,
    content_bias,
    position_bias,
    w_out,
    ln2_gain,
    ln2_bias,
    w_in,
    b_in,
    w_hid,
    b_hid,
    w_up,
    w_skip,
    m_bias,
    w_depth,
    w_point,
    p_bias,
    w_head,
    head_bias,
):
    seq_count = lax.axis_size(SEQ)
    seq_len = TOK_SEQ * seq_count
    first_pos = lax.axis_index(SEQ) * TOK_SEQ
    row_count = SEQS_DEV * TOK_SEQ
    blk_len = 512
    blk_count = seq_len // blk_len
    blk_steps = jnp.arange(blk_count, dtype=jnp.int32)
    mixer_full = (
        lax.all_gather(ln1_gain, BOTH, axis=0, tiled=True),
        lax.all_gather(ln1_bias, BOTH, axis=0, tiled=True),
        lax.all_gather(w_query, BOTH, axis=0, tiled=True),
        lax.all_gather(w_key, BOTH, axis=0, tiled=True),
        lax.all_gather(w_value, BOTH, axis=0, tiled=True),
        lax.all_gather(w_rel, BOTH, axis=1, tiled=True),
        lax.all_gather(content_bias, BOTH, axis=0, tiled=True),
        lax.all_gather(position_bias, BOTH, axis=0, tiled=True),
        lax.all_gather(w_out, BOTH, axis=0, tiled=True),
    )
    tail_full = (
        lax.all_gather(ln2_gain, BOTH, axis=0, tiled=True),
        lax.all_gather(ln2_bias, BOTH, axis=0, tiled=True),
        lax.all_gather(w_in, BOTH, axis=0, tiled=True),
        lax.all_gather(b_in, BOTH, axis=0, tiled=True),
        lax.all_gather(w_hid, BOTH, axis=0, tiled=True),
        lax.all_gather(b_hid, BOTH, axis=0, tiled=True),
        lax.all_gather(w_up, BOTH, axis=0, tiled=True),
        lax.all_gather(w_skip, BOTH, axis=0, tiled=True),
        lax.all_gather(m_bias, BOTH, axis=0, tiled=True),
        lax.all_gather(w_depth, BOTH, axis=1, tiled=True),
        lax.all_gather(w_point, BOTH, axis=0, tiled=True),
        lax.all_gather(p_bias, BOTH, axis=0, tiled=True),
        lax.all_gather(w_head, BOTH, axis=0, tiled=True),
    )
    gain_one = mixer_full[0].astype(jnp.float32)
    bias_one = mixer_full[1].astype(jnp.float32)
    query_full = mixer_full[2]
    key_full = mixer_full[3]
    value_full = mixer_full[4]
    rel_full = mixer_full[5].astype(jnp.float32).reshape(BASIS, HEADS, KEY)
    content_full = mixer_full[6].astype(jnp.float32)
    position_full = mixer_full[7].astype(jnp.float32)
    out_full = mixer_full[8]
    gain_two = tail_full[0].astype(jnp.float32)
    bias_two = tail_full[1].astype(jnp.float32)
    in_full = tail_full[2]
    in_bias = tail_full[3].astype(jnp.float32)
    hid_full = tail_full[4]
    hid_bias = tail_full[5].astype(jnp.float32)
    up_full = tail_full[6]
    skip_full = tail_full[7]
    merge_bias = tail_full[8].astype(jnp.float32)
    depth_full = tail_full[9].astype(jnp.float32)
    point_full = tail_full[10]
    point_bias = tail_full[11].astype(jnp.float32)
    head_full = tail_full[12]
    inputs_f = inputs.astype(jnp.float32).reshape(row_count, D)
    normed = layer_norm(inputs_f, gain_one, bias_one).astype(jnp.bfloat16)
    query_raw = product(normed, query_full) * 0.125
    queries = (query_raw + content_full).astype(jnp.bfloat16).reshape(SEQS_DEV, TOK_SEQ, HEADS, KEY)
    pos_in = (query_raw + position_full).reshape(row_count, HEADS, KEY)
    pos_query = (
        jnp.einsum("lhk,bhk->lhb", pos_in, rel_full, precision=HIGH)
        .astype(jnp.bfloat16)
        .reshape(SEQS_DEV, TOK_SEQ, HEADS, BASIS)
    )
    key_rows = product(normed, key_full).astype(jnp.bfloat16).reshape(SEQS_DEV, TOK_SEQ, HK)
    values = product(normed, value_full).astype(jnp.bfloat16).reshape(SEQS_DEV, TOK_SEQ, HV)
    keys_all, values_all = (
        lax.all_gather(key_rows, SEQ, axis=1, tiled=True),
        lax.all_gather(values, SEQ, axis=1, tiled=True),
    )

    def key_block(whole_rows, blk_index):
        return lax.dynamic_slice_in_dim(whole_rows, blk_index * blk_len, blk_len, 1)

    def value_block(blk_index):
        return key_block(values_all, blk_index).reshape(SEQS_DEV, blk_len, HEADS, VAL)

    def scores_at(blk_index):
        return score_block(
            queries,
            pos_query,
            key_block(keys_all, blk_index),
            first_pos,
            blk_index * blk_len,
            seq_len,
        )

    def max_step(state_pair, blk_index):
        row_max, row_sum = state_pair
        scores, basis_grid = scores_at(blk_index)
        new_max = jnp.maximum(row_max, jnp.max(scores, axis=-1))
        row_sum = row_sum * jnp.exp(row_max - new_max) + jnp.sum(
            jnp.exp(scores - new_max[..., None]), axis=-1
        )
        return ((new_max, row_sum), None)

    start_max = jnp.full((SEQS_DEV, HEADS, TOK_SEQ), -jnp.inf, jnp.float32)
    (row_max, row_sum), _ = lax.scan(max_step, (start_max, jnp.zeros_like(start_max)), blk_steps)
    log_norm = row_max + jnp.log(row_sum)

    def mix_step(mixed_sum, blk_index):
        scores, basis_grid = scores_at(blk_index)
        weights = jnp.exp(scores - log_norm[..., None]).astype(jnp.bfloat16)
        mixed_sum = mixed_sum + jnp.einsum(
            "shnc,schv->snhv", weights, value_block(blk_index), preferred_element_type=jnp.float32
        )
        return (mixed_sum, None)

    mixed_sum, _ = lax.scan(
        mix_step, jnp.zeros((SEQS_DEV, TOK_SEQ, HEADS, VAL), jnp.float32), blk_steps
    )
    attended = mixed_sum.reshape(row_count, HV).astype(jnp.bfloat16)
    resid_one = inputs_f + product(attended, out_full)
    normed_two = layer_norm(resid_one, gain_two, bias_two).astype(jnp.bfloat16)
    pre_act = product(normed_two, in_full) + in_bias
    hidden = smooth_act(pre_act).astype(jnp.bfloat16)
    lift_in = (resid_one + product(hidden, hid_full) + hid_bias).astype(jnp.bfloat16)
    lifted = product(lift_in, up_full).reshape(SEQS_DEV, TOK_SEQ, D)
    skip_rows = skips.reshape(2 * row_count, CS)
    merged = (
        jnp.repeat(lifted, 2, axis=1)
        + product(skip_rows, skip_full).reshape(SEQS_DEV, 2 * TOK_SEQ, D)
        + merge_bias
    )
    padded = with_halo(merged.astype(jnp.bfloat16), ((SEQ, 1),), 1).astype(merged.dtype)
    depth_out = (
        depth_full[0] * padded[:, :-2]
        + depth_full[1] * padded[:, 1:-1]
        + depth_full[2] * padded[:, 2:]
    ).astype(jnp.bfloat16)
    output = (
        merged
        + product(depth_out.reshape(2 * row_count, D), point_full).reshape(SEQS_DEV, 2 * TOK_SEQ, D)
        + point_bias
    )
    head_in = output.astype(jnp.bfloat16)
    head_rows = head_in.reshape(2 * row_count, D)
    logits = (product(head_rows, head_full) + head_bias.astype(jnp.float32)).reshape(
        SEQS_DEV, 2 * TOK_SEQ, TRACKS
    )
    rate_rows = jax.nn.softplus(logits)
    count_rows = counts.astype(jnp.float32)
    part_rate = jnp.sum(rate_rows, axis=1)
    part_count = jnp.sum(count_rows, axis=1)
    total_rate, total_count = lax.psum((part_rate, part_count), SEQ)
    log_total = jnp.log(total_rate)
    window_terms = jnp.sum(total_count * log_total) + 0.2 * jnp.sum(
        total_rate - total_count * log_total
    )
    local_loss = -jnp.sum(count_rows * jnp.log(rate_rows)) + jnp.where(
        lax.axis_index(SEQ) == 0, window_terms, 0.0
    )
    count_ratio = total_count / total_rate
    grad_rate = -count_rows / rate_rows + (0.2 + 0.8 * count_ratio)[:, None, :]
    grad_logit = (grad_rate * jax.nn.sigmoid(logits)).astype(jnp.bfloat16)
    bias_part = jnp.sum(grad_logit, axis=(0, 1), dtype=jnp.float32)
    loss_total, head_bias_grad = lax.psum((local_loss, bias_part), BOTH)
    loss_mean = loss_total / (SEQS_DEV * lax.axis_size(WIN) * 2 * seq_len * TRACKS)
    grad_rows = grad_logit.reshape(2 * row_count, TRACKS)
    head_grad = weight_product(head_rows, grad_rows)
    grad_out = input_product(grad_rows, head_full).astype(jnp.bfloat16)
    point_grad = weight_product(depth_out.reshape(2 * row_count, D), grad_out)
    pbias_grad = jnp.sum(grad_out, axis=0, dtype=jnp.float32)
    grad_depth = (
        input_product(grad_out, point_full).astype(jnp.bfloat16).reshape(SEQS_DEV, 2 * TOK_SEQ, D)
    )
    depth_grad = jnp.stack(
        [
            jnp.sum(grad_depth * padded[:, :-2], axis=(0, 1)),
            jnp.sum(grad_depth * padded[:, 1:-1], axis=(0, 1)),
            jnp.sum(grad_depth * padded[:, 2:], axis=(0, 1)),
        ]
    )
    depth_pad = with_halo(grad_depth, ((SEQ, 1),), 1)
    grad_merged = (
        grad_out.reshape(SEQS_DEV, 2 * TOK_SEQ, D).astype(jnp.float32)
        + depth_full[0] * depth_pad[:, 2:]
        + depth_full[1] * depth_pad[:, 1:-1]
        + depth_full[2] * depth_pad[:, :-2]
    )
    merged_low = grad_merged.astype(jnp.bfloat16)
    merged_rows = merged_low.reshape(2 * row_count, D)
    skip_weight_grad = weight_product(skip_rows, merged_rows)
    skip_grad = input_product(merged_rows, skip_full).reshape(SEQS_DEV, 2 * TOK_SEQ, CS)
    mbias_grad = jnp.sum(merged_rows, axis=0, dtype=jnp.float32)
    lift_grad = (
        jnp.sum(merged_low.reshape(SEQS_DEV, TOK_SEQ, 2, D), axis=2, dtype=jnp.float32)
        .reshape(row_count, D)
        .astype(jnp.bfloat16)
    )
    up_grad = weight_product(lift_in, lift_grad)
    grad_two = input_product(lift_grad, up_full).astype(jnp.bfloat16)
    hid_grad = weight_product(hidden, grad_two)
    hbias_grad = jnp.sum(grad_two, axis=0, dtype=jnp.float32)
    grad_hidden = input_product(grad_two, hid_full).astype(jnp.bfloat16)
    _, pull_act = jax.vjp(smooth_act, pre_act)
    grad_pre = pull_act(grad_hidden.astype(jnp.float32))[0].astype(jnp.bfloat16)
    in_grad = weight_product(normed_two, grad_pre)
    ibias_grad = jnp.sum(grad_pre, axis=0, dtype=jnp.float32)
    _, pull_two = jax.vjp(layer_norm, resid_one, gain_two, bias_two)
    grad_resid, gain_two_grad, bias_two_grad = pull_two(input_product(grad_pre, in_full))
    grad_one = (grad_two.astype(jnp.float32) + grad_resid).astype(jnp.bfloat16)
    out_grad = weight_product(attended, grad_one)
    grad_att = (
        input_product(grad_one, out_full)
        .astype(jnp.bfloat16)
        .reshape(SEQS_DEV, TOK_SEQ, HEADS, VAL)
    )

    def grad_parts(blk_index):
        key_blk = key_block(keys_all, blk_index)
        scores, basis_grid = score_block(
            queries, pos_query, key_blk, first_pos, blk_index * blk_len, seq_len
        )
        soft_probs = jnp.exp(scores - log_norm[..., None])
        prob_grad = jnp.einsum(
            "snhv,schv->shnc", grad_att, value_block(blk_index), preferred_element_type=jnp.float32
        )
        return (key_blk, basis_grid, soft_probs, prob_grad)

    def delta_step(delta_sum, blk_index):
        key_blk, basis_grid, soft_probs, prob_grad = grad_parts(blk_index)
        return (delta_sum + jnp.sum(soft_probs * prob_grad, axis=-1), None)

    row_delta, _ = lax.scan(
        delta_step, jnp.zeros((SEQS_DEV, HEADS, TOK_SEQ), jnp.float32), blk_steps
    )

    def query_terms(state_pair, blk_index):
        key_blk, basis_grid, soft_probs, prob_grad = grad_parts(blk_index)
        score_grad = (soft_probs * (prob_grad - row_delta[..., None])).astype(jnp.bfloat16)
        key_heads = key_blk.reshape(SEQS_DEV, blk_len, HEADS, KEY)
        query_acc = state_pair[0] + jnp.einsum(
            "shnc,schk->snhk", score_grad, key_heads, preferred_element_type=jnp.float32
        )
        pos_acc = state_pair[1] + jnp.einsum(
            "shnc,ncb->snhb", score_grad, basis_grid, preferred_element_type=jnp.float32
        )
        return ((query_acc, pos_acc), score_grad, soft_probs)

    query_zero = jnp.zeros((SEQS_DEV, TOK_SEQ, HEADS, KEY), jnp.float32)
    pos_zero = jnp.zeros((SEQS_DEV, TOK_SEQ, HEADS, BASIS), jnp.float32)

    def sum_step(state_four, blk_index):
        pair_next, score_grad, soft_probs = query_terms((state_four[0], state_four[1]), blk_index)
        key_part = jnp.einsum(
            "shnc,snhk->schk", score_grad, queries, preferred_element_type=jnp.float32
        ).reshape(SEQS_DEV, blk_len, HK)
        value_part = jnp.einsum(
            "shnc,snhv->schv",
            soft_probs.astype(jnp.bfloat16),
            grad_att,
            preferred_element_type=jnp.float32,
        ).reshape(SEQS_DEV, blk_len, HV)
        key_acc = lax.dynamic_update_slice_in_dim(state_four[2], key_part, blk_index * blk_len, 1)
        value_acc = lax.dynamic_update_slice_in_dim(
            state_four[3], value_part, blk_index * blk_len, 1
        )
        return ((pair_next[0], pair_next[1], key_acc, value_acc), None)

    start_four = (
        query_zero,
        pos_zero,
        jnp.zeros((SEQS_DEV, seq_len, HK), jnp.float32),
        jnp.zeros((SEQS_DEV, seq_len, HV), jnp.float32),
    )
    (query_acc, pos_acc, key_terms_all, value_terms_all), _ = lax.scan(
        sum_step, start_four, blk_steps
    )
    key_sum, value_sum = (
        lax.psum_scatter(
            key_terms_all.astype(jnp.bfloat16), SEQ, scatter_dimension=1, tiled=True
        ).astype(jnp.float32),
        lax.psum_scatter(
            value_terms_all.astype(jnp.bfloat16), SEQ, scatter_dimension=1, tiled=True
        ).astype(jnp.float32),
    )
    key_grad = key_sum.reshape(row_count, HK).astype(jnp.bfloat16)
    value_grad = value_sum.reshape(row_count, HV).astype(jnp.bfloat16)
    query_low = query_acc.astype(jnp.bfloat16).reshape(row_count, HK)
    content_grad = jnp.sum(query_low, axis=0, dtype=jnp.float32)
    pos_low = pos_acc.astype(jnp.bfloat16).reshape(row_count, HEADS, BASIS).astype(jnp.float32)
    pos_in_grad = jnp.einsum("lhb,bhk->lhk", pos_low, rel_full, precision=HIGH)
    rel_grad = jnp.einsum("lhb,lhk->bhk", pos_low, pos_in, precision=HIGH).reshape(BASIS, HK)
    position_grad = jnp.sum(pos_in_grad, axis=0).reshape(HK)
    query_grad = (
        0.125 * (query_low.astype(jnp.float32) + pos_in_grad.reshape(row_count, HK))
    ).astype(jnp.bfloat16)
    wq_grad = weight_product(normed, query_grad)
    wk_grad = weight_product(normed, key_grad)
    wv_grad = weight_product(normed, value_grad)
    grad_normed = (
        input_product(query_grad, query_full)
        + input_product(key_grad, key_full)
        + input_product(value_grad, value_full)
    )
    _, pull_one = jax.vjp(layer_norm, inputs_f, gain_one, bias_one)
    grad_norm_in, gain_one_grad, bias_one_grad = pull_one(grad_normed)
    grad_inputs = (grad_one.astype(jnp.float32) + grad_norm_in).reshape(SEQS_DEV, TOK_SEQ, D)
    mixer_grads = (
        lax.psum_scatter(gain_one_grad, BOTH, scatter_dimension=0, tiled=True),
        lax.psum_scatter(bias_one_grad, BOTH, scatter_dimension=0, tiled=True),
        lax.psum_scatter(wq_grad, BOTH, scatter_dimension=0, tiled=True),
        lax.psum_scatter(wk_grad, BOTH, scatter_dimension=0, tiled=True),
        lax.psum_scatter(wv_grad, BOTH, scatter_dimension=0, tiled=True),
        lax.psum_scatter(rel_grad, BOTH, scatter_dimension=1, tiled=True),
        lax.psum_scatter(content_grad, BOTH, scatter_dimension=0, tiled=True),
        lax.psum_scatter(position_grad, BOTH, scatter_dimension=0, tiled=True),
        lax.psum_scatter(out_grad, BOTH, scatter_dimension=0, tiled=True),
    )
    tail_grads = (
        lax.psum_scatter(gain_two_grad, BOTH, scatter_dimension=0, tiled=True),
        lax.psum_scatter(bias_two_grad, BOTH, scatter_dimension=0, tiled=True),
        lax.psum_scatter(in_grad, BOTH, scatter_dimension=0, tiled=True),
        lax.psum_scatter(ibias_grad, BOTH, scatter_dimension=0, tiled=True),
        lax.psum_scatter(hid_grad, BOTH, scatter_dimension=0, tiled=True),
        lax.psum_scatter(hbias_grad, BOTH, scatter_dimension=0, tiled=True),
        lax.psum_scatter(up_grad, BOTH, scatter_dimension=0, tiled=True),
        lax.psum_scatter(skip_weight_grad, BOTH, scatter_dimension=0, tiled=True),
        lax.psum_scatter(mbias_grad, BOTH, scatter_dimension=0, tiled=True),
        lax.psum_scatter(depth_grad, BOTH, scatter_dimension=1, tiled=True),
        lax.psum_scatter(point_grad, BOTH, scatter_dimension=0, tiled=True),
        lax.psum_scatter(pbias_grad, BOTH, scatter_dimension=0, tiled=True),
        lax.psum_scatter(head_grad, BOTH, scatter_dimension=0, tiled=True),
    )
    return (
        (loss_mean, head_in, grad_inputs, skip_grad)
        + tuple(mixer_grads)
        + tuple(tail_grads)
        + (head_bias_grad,)
    )


SPLIT, ROWED, TILED = P(BOTH), P(BOTH, None), P(WIN, SEQ, None)


def solution(mesh):
    paired = mesh.shape[WIN] == 8 and mesh.shape[SEQ] == 4
    return jax.shard_map(
        split_body if paired else general_body,
        mesh=mesh,
        in_specs=(
            TILED,
            TILED,
            TILED,
            SPLIT,
            SPLIT,
            ROWED,
            ROWED,
            ROWED,
            P(None, BOTH),
            SPLIT,
            SPLIT,
            ROWED,
            SPLIT,
            SPLIT,
            ROWED,
            SPLIT,
            ROWED,
            SPLIT,
            ROWED,
            ROWED,
            SPLIT,
            P(None, BOTH),
            ROWED,
            SPLIT,
            ROWED,
            P(),
        ),
        out_specs=(
            P(),
            TILED,
            TILED,
            TILED,
            SPLIT,
            SPLIT,
            ROWED,
            ROWED,
            ROWED,
            P(None, BOTH),
            SPLIT,
            SPLIT,
            ROWED,
            SPLIT,
            SPLIT,
            ROWED,
            SPLIT,
            ROWED,
            SPLIT,
            ROWED,
            ROWED,
            SPLIT,
            P(None, BOTH),
            ROWED,
            SPLIT,
            ROWED,
            P(),
        ),
        check_vma=False,
    )
```

```python
import functools
import math

import jax
import jax.numpy as jnp
from jax import lax
from jax.experimental import pallas as pl
from jax.experimental.pallas import tpu as pltpu
from jax.sharding import PartitionSpec as P

D = 1536
HEADS = 8
KEY = 64
VAL = 192
BASIS = 32
CS = 1280
TRACKS = 2608
TOK_SEQ = 256
SEQS_DEV = 1
HK = 512
HV = 1536


WIN, SEQ = "win", "seq"
BOTH = (WIN, SEQ)
EPS = 1e-05
HIGH = lax.Precision.HIGHEST


def with_halo(cells, sides, width):
    for axis, dim in sides:
        count = lax.axis_size(axis)
        ends = count - 1
        head = lax.slice_in_dim(cells, 0, width, axis=dim)
        tail = lax.slice_in_dim(cells, cells.shape[dim] - width, cells.shape[dim], axis=dim)
        cells = jnp.concatenate(
            [
                lax.ppermute(tail, axis, [(i, (i + 1) % count) for i in range(ends)]),
                cells,
                lax.ppermute(head, axis, [((i + 1) % count, i) for i in range(ends)]),
            ],
            axis=dim,
        )
    return cells


def basis_table(offsets, seq_len, basis_count):
    halves = basis_count // 2
    ramped = jnp.arange(halves, dtype=jnp.int32).astype(jnp.float32) / (halves - 1)
    half_life = 3.0 * jnp.exp(ramped * math.log(seq_len / 3.0))
    distance = jnp.abs(offsets)[..., None]
    decays = jnp.exp(-math.log(2.0) * distance / half_life)
    return jnp.concatenate([decays, jnp.sign(offsets)[..., None] * decays], axis=-1)


def layer_norm(values, gain_row, bias_row):
    centred = values - jnp.mean(values, axis=-1, keepdims=True)
    spread = jnp.mean(centred * centred, axis=-1, keepdims=True)
    return centred * lax.rsqrt(spread + EPS) * gain_row + bias_row


def smooth_act(values):
    return jax.nn.gelu(values, approximate=True)


def product(first_arg, second_arg):
    return jnp.dot(first_arg, second_arg, preferred_element_type=jnp.float32)


def weight_product(first_arg, second_arg):
    return lax.dot_general(
        first_arg, second_arg, (((0,), (0,)), ((), ())), preferred_element_type=jnp.float32
    )


def input_product(first_arg, second_arg):
    return lax.dot_general(
        first_arg, second_arg, (((1,), (1,)), ((), ())), preferred_element_type=jnp.float32
    )


def score_block(query_blk, pos_blk, key_blk, query_first, key_first, seq_len):
    row_pos = query_first + jnp.arange(query_blk.shape[1], dtype=jnp.int32)
    col_pos = key_first + jnp.arange(key_blk.shape[1], dtype=jnp.int32)
    offsets = (row_pos[:, None] - col_pos[None, :]).astype(jnp.float32)
    basis_grid = basis_table(offsets, seq_len, BASIS).astype(jnp.bfloat16)
    key_heads = key_blk.reshape(key_blk.shape[0], key_blk.shape[1], HEADS, KEY)
    content = jnp.einsum(
        "snhk,schk->shnc", query_blk, key_heads, preferred_element_type=jnp.float32
    )
    position = jnp.einsum("snhb,ncb->shnc", pos_blk, basis_grid, preferred_element_type=jnp.float32)
    return (content + position, basis_grid)


F32 = jnp.float32
LOW = jnp.bfloat16
ROWS = 256
FF = 3072
RANKS = 4
WINDOWS = 8


def wide_table(seq_len):
    offsets = (seq_len - 1 - jnp.arange(2 * seq_len, dtype=jnp.int32)).astype(F32)
    return basis_table(offsets, seq_len, BASIS).astype(LOW).T


def offset_window(table_ref, keys):
    start = keys - ROWS - pl.program_id(0) * ROWS
    return table_ref[:, pl.ds(pl.multiple_of(start, 128), keys + ROWS)]


def row_scores(query, key, pos_query, window):
    keys = key.shape[0]
    wide = product(pos_query, window)
    lined = pltpu.roll(wide, keys + 1, 1, stride=1, stride_axis=0)
    return input_product(query, key) + lined[:, :keys]


def head_columns(head):
    return (
        slice(head * KEY, (head + 1) * KEY),
        slice(head * VAL, (head + 1) * VAL),
        slice(head * BASIS, (head + 1) * BASIS),
    )


def mix_kernel(heads, q_ref, k_ref, v_ref, pos_ref, table_ref, out_ref, norm_ref):
    window = offset_window(table_ref, k_ref.shape[0])
    for head in range(heads):
        ks, vs, bs = head_columns(head)
        scores = row_scores(q_ref[:, ks], k_ref[:, ks], pos_ref[:, bs], window)
        top = jnp.max(scores, axis=1, keepdims=True)
        powers = jnp.exp(scores - top)
        total = jnp.sum(powers, axis=1, keepdims=True)
        weights = (powers * (1.0 / total)).astype(LOW)
        out_ref[:, vs] = product(weights, v_ref[:, vs]).astype(LOW)
        norm_ref[:, head : head + 1] = top + jnp.log(total)


def mix_grad_kernel(
    heads,
    q_ref,
    k_ref,
    v_ref,
    pos_ref,
    table_ref,
    norm_ref,
    ga_ref,
    dq_ref,
    dpos_ref,
    dk_ref,
    dv_ref,
    dk_sum,
    dv_sum,
):
    step = pl.program_id(0)
    keys = k_ref.shape[0]
    window = offset_window(table_ref, keys)
    down = lax.broadcasted_iota(jnp.int32, (ROWS, ROWS), 0)
    across = lax.broadcasted_iota(jnp.int32, (ROWS, ROWS), 1)
    flip = (down + across == ROWS - 1).astype(LOW)

    @pl.when(step == 0)
    def _():
        dk_sum[...] = jnp.zeros_like(dk_sum)
        dv_sum[...] = jnp.zeros_like(dv_sum)

    for head in range(heads):
        ks, vs, bs = head_columns(head)
        query, key, value, grad = q_ref[:, ks], k_ref[:, ks], v_ref[:, vs], ga_ref[:, vs]
        scores = row_scores(query, key, pos_ref[:, bs], window)
        probs = jnp.exp(scores - norm_ref[:, head : head + 1])
        dprob = input_product(grad, value)
        delta = jnp.sum(probs * dprob, axis=1, keepdims=True)
        dscore = (probs * (dprob - delta)).astype(LOW)
        dq_ref[:, ks] = product(dscore, key).astype(LOW)
        dk_sum[:, ks] += weight_product(dscore, query)
        dv_sum[:, vs] += weight_product(probs.astype(LOW), grad)
        wide = jnp.concatenate([product(flip, dscore), jnp.zeros((ROWS, ROWS), F32)], axis=1)
        lined = pltpu.roll(wide, 0, 1, stride=1, stride_axis=0).astype(LOW)
        turned = input_product(lined, window).astype(LOW)
        dpos_ref[:, bs] = product(flip, turned).astype(LOW)

    @pl.when(step == pl.num_programs(0) - 1)
    def _():
        dk_ref[...] = dk_sum[...].astype(LOW)
        dv_ref[...] = dv_sum[...].astype(LOW)


def row_spec(array):
    return pl.BlockSpec((ROWS, array.shape[1]), lambda i: (i, 0))


def whole_spec(array):
    return pl.BlockSpec(array.shape, lambda i: (0, 0))


def mix(query, key, value, pos_query, table):
    rows, keys = query.shape[0], key.shape[0]
    heads = key.shape[1] // KEY
    norm = jax.ShapeDtypeStruct((rows, heads), F32)
    out = jax.ShapeDtypeStruct((rows, value.shape[1]), LOW)
    return pl.pallas_call(
        functools.partial(mix_kernel, heads),
        grid=(rows // ROWS,),
        in_specs=[
            row_spec(query),
            whole_spec(key),
            whole_spec(value),
            row_spec(pos_query),
            whole_spec(table),
        ],
        out_specs=[row_spec(out), row_spec(norm)],
        out_shape=[out, norm],
        compiler_params=pltpu.CompilerParams(vmem_limit_bytes=40 * 2**20),
        cost_estimate=pl.CostEstimate(
            flops=10**10, transcendentals=rows * keys * heads, bytes_accessed=4 * 2**20
        ),
    )(query, key, value, pos_query, table)


def mix_grad(query, key, value, pos_query, table, norm, grad):
    rows, keys = query.shape[0], key.shape[0]
    heads = key.shape[1] // KEY

    def like(array):
        return jax.ShapeDtypeStruct(array.shape, LOW)

    return pl.pallas_call(
        functools.partial(mix_grad_kernel, heads),
        grid=(rows // ROWS,),
        in_specs=[
            row_spec(query),
            whole_spec(key),
            whole_spec(value),
            row_spec(pos_query),
            whole_spec(table),
            row_spec(norm),
            row_spec(grad),
        ],
        out_specs=[row_spec(query), row_spec(pos_query), whole_spec(key), whole_spec(value)],
        out_shape=[like(query), like(pos_query), like(key), like(value)],
        scratch_shapes=[pltpu.VMEM(key.shape, F32), pltpu.VMEM(value.shape, F32)],
        compiler_params=pltpu.CompilerParams(vmem_limit_bytes=40 * 2**20),
        cost_estimate=pl.CostEstimate(
            flops=15 * 10**9, transcendentals=rows * keys * heads, bytes_accessed=6 * 2**20
        ),
    )(query, key, value, pos_query, table, norm, grad)


def trade(block, axis, bits):
    count = lax.axis_size(axis)
    return lax.ppermute(block, axis, [(i, i ^ bits) for i in range(count)])


def in_order(pieces, index):
    pieces = list(pieces)
    bit = 1
    while bit < len(pieces):
        odd = (index & bit) != 0
        pieces = [jnp.where(odd, pieces[k ^ bit], pieces[k]) for k in range(len(pieces))]
        bit *= 2
    return pieces


def place_kernel(axis, shift, inner, columns, *refs):
    index = lax.axis_index(axis)
    index = index // shift if shift > 1 else index
    count = len(refs) - 1
    out_ref = refs[count]
    for k in range(count):
        to = (index % count) ^ k
        if columns:
            width = refs[k].shape[1]
            out_ref[:, pl.ds(pl.multiple_of(to * width, 128), width)] = refs[k][...]
        elif inner:
            for outer in range(inner):
                out_ref[outer, to] = refs[k][outer]
        else:
            out_ref[to] = refs[k][...]


def place(pieces, axis, shift=1, inner=0, columns=False):
    count, shape = len(pieces), pieces[0].shape
    if columns:
        shape = (shape[0], count * shape[1])
    elif inner:
        shape = (inner, count) + shape[1:]
    else:
        shape = (count,) + shape
    return pl.pallas_call(
        functools.partial(place_kernel, axis, shift, inner, columns),
        out_shape=jax.ShapeDtypeStruct(shape, pieces[0].dtype),
        compiler_params=pltpu.CompilerParams(vmem_limit_bytes=24 * 2**20),
        cost_estimate=pl.CostEstimate(flops=0, transcendentals=0, bytes_accessed=1024),
    )(*pieces)


def pick(blocks, index):
    return lax.dynamic_index_in_dim(blocks, index, 0, keepdims=False)


tie = lax.optimization_barrier


class Flow:
    def __init__(self, stages):
        self.stages, self.result = stages, None
        self.pending = next(stages)

    def step(self, arrived):
        try:
            self.pending = self.stages.send(arrived)
        except StopIteration as last:
            self.pending, self.result = (), last.value


def advance(values, *flows):
    values, arrived = tie((tie(values), [flow.pending for flow in flows]))
    for flow, rows in zip(flows, arrived):
        flow.step(rows)
    return values


def seq_all(rows):
    near, far = yield trade(rows, SEQ, 1), trade(rows, SEQ, 2)
    last = yield trade(far, SEQ, 1)
    return place([rows, near, far, last], SEQ).reshape(RANKS * rows.shape[0], rows.shape[1])


def seq_sum(partial, rank):
    blocks = partial.reshape(RANKS, ROWS, partial.shape[1])
    sent = jnp.stack([pick(blocks, rank ^ 1), pick(blocks, rank ^ 3)]).astype(LOW)
    got = yield trade(sent, SEQ, 1)
    last = yield trade((pick(blocks, rank ^ 2) + got[1].astype(F32)).astype(LOW), SEQ, 2)
    return pick(blocks, rank) + got[0].astype(F32) + last.astype(F32)


def seq_swap(blocks, rank):
    got = yield [trade(pick(blocks, rank ^ k), SEQ, k) for k in range(1, RANKS)]
    return [pick(blocks, rank)] + got


def seq_swap_two(blocks, rank):
    far = yield trade(jnp.stack([pick(blocks, rank ^ 2), pick(blocks, rank ^ 3)]), SEQ, 2)
    near = yield trade(jnp.stack([pick(blocks, rank ^ 1), far[1]]), SEQ, 1)
    return [pick(blocks, rank), near[0], far[0], near[1]]


def deal_kernel(parts, whole_ref, dealt_ref):
    width = whole_ref.shape[1] // (RANKS * parts)
    for t in range(RANKS):
        for p in range(parts):
            first = (p * RANKS + t) * width
            dealt_ref[t, :, p * width : (p + 1) * width] = whole_ref[:, first : first + width]


def deal(array, parts):
    rows, columns = array.shape
    return pl.pallas_call(
        functools.partial(deal_kernel, parts),
        out_shape=jax.ShapeDtypeStruct((RANKS, rows, columns // RANKS), array.dtype),
    )(array)


def undeal_kernel(parts, *refs):
    rank = lax.axis_index(SEQ)
    width = refs[0].shape[1] // parts
    pieces = [ref[...].astype(F32) for ref in refs[:RANKS]]
    for bit in (1, 2):
        odd = (rank & bit) != 0
        pieces = [jnp.where(odd, pieces[k ^ bit], pieces[k]) for k in range(RANKS)]
    for t in range(RANKS):
        for p in range(parts):
            first = (p * RANKS + t) * width
            refs[RANKS][:, first : first + width] = pieces[t][:, p * width : (p + 1) * width]


def undeal(pieces, parts):
    rows, columns = pieces[0].shape
    return pl.pallas_call(
        functools.partial(undeal_kernel, parts),
        out_shape=jax.ShapeDtypeStruct((rows, columns * RANKS), F32),
    )(*pieces)


ROOM = 640
EXTRA = 8
SHORT = {}
for _name, _size in (
    ("gain1", 48),
    ("bias1", 48),
    ("gain2", 48),
    ("bias2", 48),
    ("b_in", 96),
    ("b_hid", 48),
    ("m", 48),
    ("p", 48),
    ("d0", 48),
    ("d1", 48),
    ("d2", 48),
    ("con", 16),
    ("pos", 16),
):
    _first = sum(_high - _low for _low, _high in SHORT.values())
    SHORT[_name] = (_first, _first + _size)
DEVICES = WINDOWS * RANKS
REL = HK // DEVICES


def pack_kernel(names, *refs):
    out_ref = refs[-1]
    out_ref[...] = jnp.zeros_like(out_ref)
    for name, ref in zip(names, refs):
        low, high = SHORT[name]
        out_ref[0:1, low:high] = ref[...].astype(F32)
    for b in range(BASIS):
        out_ref[1:2, b * REL : (b + 1) * REL] = refs[-2][b : b + 1, :].astype(F32)


def pack(rows, rel):
    return pl.pallas_call(
        functools.partial(pack_kernel, tuple(rows)),
        out_shape=jax.ShapeDtypeStruct((EXTRA, ROOM), F32),
    )(*(row[None] for row in rows.values()), rel)


WIDE = ("gain1", "bias1", "gain2", "bias2", "b_hid", "m", "p", "d0", "d1", "d2")


def unpack_kernel(table_ref, wide_ref, in_ref, con_ref, pos_ref, rel_ref):
    rank = lax.axis_index(SEQ)
    for d in range(DEVICES):
        line = table_ref[d][0:1]
        for number, name in enumerate(WIDE):
            low, high = SHORT[name]
            wide_ref[number : number + 1, d * 48 : (d + 1) * 48] = line[:, low:high]
    low, high = SHORT["b_in"]
    for w in range(WINDOWS):
        in_ref[0:1, w * 96 : (w + 1) * 96] = table_ref[RANKS * w + rank][0:1, low:high]
    here = DEVICES // RANKS
    for j in range(here):
        block = table_ref[here * rank + j]
        columns = slice(j * REL, (j + 1) * REL)
        for ref, name in ((con_ref, "con"), (pos_ref, "pos")):
            low, high = SHORT[name]
            ref[0:1, columns] = block[0:1, low:high]
        for b in range(BASIS):
            rel_ref[b : b + 1, columns] = block[1:2, b * REL : (b + 1) * REL]


def unpack(table):
    hq = HK // RANKS
    shapes = ((16, D), (1, FF // RANKS), (1, hq), (1, hq), (BASIS, hq))
    return pl.pallas_call(
        unpack_kernel, out_shape=[jax.ShapeDtypeStruct(shape, F32) for shape in shapes]
    )(table)


def pack_grads_kernel(names, *refs):
    rank = lax.axis_index(SEQ)
    wide, (in_ref, con_ref, pos_ref, rel_ref, out_ref) = refs[:-5], refs[-5:]
    out_ref[...] = jnp.zeros_like(out_ref)
    for d in range(DEVICES):
        for name, ref in zip(names, wide):
            low, high = SHORT[name]
            out_ref[d, 0:1, low:high] = ref[0:1, d * 48 : (d + 1) * 48]
    low, high = SHORT["b_in"]
    for w in range(WINDOWS):
        out_ref[RANKS * w + rank, 0:1, low:high] = in_ref[0:1, w * 96 : (w + 1) * 96]
    here = DEVICES // RANKS
    for j in range(here):
        columns = slice(j * REL, (j + 1) * REL)
        for ref, name in ((con_ref, "con"), (pos_ref, "pos")):
            low, high = SHORT[name]
            out_ref[here * rank + j, 0:1, low:high] = ref[0:1, columns]
        for b in range(BASIS):
            out_ref[here * rank + j, 1:2, b * REL : (b + 1) * REL] = rel_ref[
                b : b + 1, columns
            ]


def pack_grads(rows, in_row, con, pos, rel):
    return pl.pallas_call(
        functools.partial(pack_grads_kernel, tuple(rows)),
        out_shape=jax.ShapeDtypeStruct((DEVICES, EXTRA, ROOM), F32),
    )(*(row.reshape(1, -1) for row in rows.values()), in_row[None], con[None], pos[None], rel)


def finish_kernel(hq, hv, height, *refs):
    rank = lax.axis_index(SEQ)
    pieces, (q_ref, k_ref, v_ref, short_ref, rel_ref) = refs[:RANKS], refs[RANKS:]
    extra = jnp.zeros((EXTRA, ROOM), F32)
    for k in range(RANKS):
        block = pieces[k][...].astype(F32)
        t = rank ^ k
        weights = block[:height]
        narrow = pl.ds(pl.multiple_of(t * hq, 128), hq)
        q_ref[:, narrow] = weights[:, :hq]
        k_ref[:, narrow] = weights[:, hq : 2 * hq]
        v_ref[:, pl.ds(pl.multiple_of(t * hv, 128), hv)] = weights[:, 2 * hq :]
        extra = extra + block[height:]
    short_ref[...] = extra[0:1]
    for b in range(BASIS):
        rel_ref[b : b + 1, :] = extra[1:2, b * REL : (b + 1) * REL]


def finish(pieces, hq, hv):
    height = pieces[0].shape[0] - EXTRA
    shapes = ((height, HK), (height, HK), (height, HV), (1, ROOM), (BASIS, REL))
    return pl.pallas_call(
        functools.partial(finish_kernel, hq, hv, height),
        out_shape=[jax.ShapeDtypeStruct(shape, F32) for shape in shapes],
    )(*pieces)


def edges(rows, axis):
    count = lax.axis_size(axis)
    below, above = yield (
        lax.ppermute(rows[-1:], axis, [(i, i + 1) for i in range(count - 1)]),
        lax.ppermute(rows[:1], axis, [(i + 1, i) for i in range(count - 1)]),
    )
    return jnp.concatenate([below, rows, above], axis=0)


def win_all(block):
    got = yield [trade(block, WIN, 2 * k) for k in range(1, WINDOWS // 2)]
    column = place([block] + got, WIN, 2)
    beside = yield trade(column, WIN, 1)
    both = place([column, beside], WIN, 1, WINDOWS // 2)
    return both.reshape((WINDOWS,) + block.shape)


def z_sum(column, z):
    got = yield trade(jnp.stack([pick(column, z ^ 1), pick(column, z ^ 3)]), WIN, 2)
    last = yield trade(plus(pick(column, z ^ 2), got[1]), WIN, 4)
    return pick(column, z).astype(F32) + got[0].astype(F32) + last.astype(F32)


def win_sum(kept, sent, window):
    got = yield trade(sent, WIN, 1)
    total = yield from z_sum(plus(kept, got), window // 2)
    return total


def shared_sum(row):
    for axis, bits in ((WIN, 1), (WIN, 2), (WIN, 4), (SEQ, 1), (SEQ, 2)):
        got = yield trade(row, axis, bits)
        row = row + got
    return row


def split_kernel(axis, height, first_ref, second_ref, kept_ref, sent_ref):
    grads = weight_product(first_ref[...], second_ref[...]).astype(LOW)
    odd = lax.axis_index(axis) % 2
    for pair in range(kept_ref.shape[0]):
        low = 2 * pair * height
        even_rows = grads[low : low + height]
        odd_rows = grads[low + height : low + 2 * height]

        @pl.when(odd == 0)
        def _():
            kept_ref[pair] = even_rows
            sent_ref[pair] = odd_rows

        @pl.when(odd == 1)
        def _():
            kept_ref[pair] = odd_rows
            sent_ref[pair] = even_rows


def split_product(first_arg, second_arg, axis, height):
    depth, rows = first_arg.shape
    columns = second_arg.shape[1]
    width = 384 if rows % 384 == 0 else 640
    pairs = width // (2 * height)
    out = jax.ShapeDtypeStruct((rows // (2 * height), height, columns), LOW)
    out_spec = pl.BlockSpec((pairs, height, columns), lambda i: (i, 0, 0))
    return pl.pallas_call(
        functools.partial(split_kernel, axis, height),
        grid=(rows // width,),
        in_specs=[pl.BlockSpec((depth, width), lambda i: (0, i)), whole_spec(second_arg)],
        out_specs=[out_spec, out_spec],
        out_shape=[out, out],
        compiler_params=pltpu.CompilerParams(vmem_limit_bytes=32 * 2**20),
        cost_estimate=pl.CostEstimate(
            flops=2 * depth * rows * columns,
            transcendentals=0,
            bytes_accessed=2 * (depth * rows + depth * columns + rows * columns),
        ),
    )(first_arg, second_arg)


def core_sum(first_arg, second_arg):
    height = first_arg.shape[1] // DEVICES
    kept, sent = split_product(first_arg, second_arg, SEQ, height)
    got = yield trade(sent, SEQ, 1)
    return plus(kept, got).reshape((4, 2, 2) + kept.shape[1:])


def plus(first_arg, *others):
    total = first_arg.astype(F32)
    for other in others:
        total = total + other.astype(F32)
    return total.astype(LOW)


def chip_sum(grads, rank, window, y_first):
    z, y = window // 2, window % 2
    x = rank // 2
    heights = [g.shape[3] for g in grads]

    def half(index):
        axis = 1 if y_first else 2
        cut = [lax.dynamic_index_in_dim(g, index, axis, keepdims=False) for g in grads]
        return cut[0] if len(cut) == 1 else jnp.concatenate(cut, axis=2)

    def quarter(both, index):
        return lax.dynamic_index_in_dim(both, index, 1, keepdims=False)

    first, second = (y, x) if y_first else (x, y)
    steps = ((WIN, 1), (SEQ, 2)) if y_first else ((SEQ, 2), (WIN, 1))
    got = yield trade(half(1 - first), *steps[0])
    both = plus(half(first), got)
    got = yield trade(quarter(both, 1 - second), *steps[1])
    total = yield from z_sum(plus(quarter(both, second), got), z)
    results, low = [], 0
    for height in heights:
        results.append(total[low : low + height])
        low += height
    return results


def split_body(
    inputs,
    skips,
    counts,
    ln1_gain,
    ln1_bias,
    w_query,
    w_key,
    w_value,
    w_rel,
    content_bias,
    position_bias,
    w_out,
    ln2_gain,
    ln2_bias,
    w_in,
    b_in,
    w_hid,
    b_hid,
    w_up,
    w_skip,
    m_bias,
    w_depth,
    w_point,
    p_bias,
    w_head,
    head_bias,
):
    window, rank = lax.axis_index(WIN), lax.axis_index(SEQ)
    seq_len = ROWS * RANKS
    hq, hv, ff = HK // RANKS, HV // RANKS, FF // RANKS

    packed = pack(
        {
            "gain1": ln1_gain,
            "bias1": ln1_bias,
            "gain2": ln2_gain,
            "bias2": ln2_bias,
            "b_in": b_in,
            "b_hid": b_hid,
            "m": m_bias,
            "p": p_bias,
            "d0": w_depth[0],
            "d1": w_depth[1],
            "d2": w_depth[2],
            "con": content_bias,
            "pos": position_bias,
        },
        w_rel,
    ).astype(LOW)
    qkv_local = jnp.stack(
        [
            jnp.concatenate(
                [
                    jnp.concatenate(
                        [
                            w_query[:, t * hq : (t + 1) * hq],
                            w_key[:, t * hq : (t + 1) * hq],
                            w_value[:, t * hv : (t + 1) * hv],
                        ],
                        axis=1,
                    ),
                    packed,
                ]
            )
            for t in range(RANKS)
        ]
    )
    qkv_flow = Flow(seq_swap(qkv_local, rank))
    four = lax.all_gather(jnp.concatenate([w_out, w_up, w_skip, w_point]), BOTH, axis=0)
    inputs_own, w_in, w_hid = advance((inputs.reshape(ROWS, D), w_in, w_hid), qkv_flow)
    qkv_flow = Flow(win_all(place(qkv_flow.result, SEQ).reshape(-1, ROOM)))
    inputs_flow = Flow(seq_all(inputs_own))
    dealt, w_hid, w_head = advance((deal(w_in, WINDOWS), w_hid, w_head), qkv_flow, inputs_flow)
    in_flow = Flow(seq_swap(dealt, rank))
    hid_flow = Flow(win_all(w_hid))
    head_full = lax.all_gather(w_head, BOTH, axis=0, tiled=True)
    advance((), qkv_flow, in_flow, inputs_flow)
    gathered = qkv_flow.result.reshape(DEVICES, -1, ROOM)
    height = gathered.shape[1] - EXTRA
    qkv_part = gathered[:, :height].reshape(D, ROOM)
    wide, in_bias, content, position, rel_part, qkv_part, inputs_all, in_rows = advance(
        (
            *unpack(gathered[:, height:].astype(F32)),
            qkv_part,
            inputs_flow.result,
            place(in_flow.result, SEQ).reshape(-1, ff),
        ),
        hid_flow,
    )
    in_flow = Flow(win_all(in_rows))
    row_of = {name: wide[number] for number, name in enumerate(WIDE)}
    depth_full = [row_of[name] for name in ("d0", "d1", "d2")]
    heads_here = hq // KEY
    same_head = (
        jnp.arange(hq)[:, None] // KEY == jnp.arange(heads_here * BASIS)[None, :] // BASIS
    )
    rel_square = jnp.where(same_head, jnp.tile(rel_part.T, (1, heads_here)), 0.0)
    gain_one, bias_one = row_of["gain1"], row_of["bias1"]
    gain_two, bias_two = row_of["gain2"], row_of["bias2"]

    normed = layer_norm(inputs_all.astype(F32), gain_one, bias_one).astype(LOW)
    projected = product(normed, qkv_part)
    query_raw = projected[:, :hq] * 0.125
    queries = (query_raw + content).astype(LOW)
    pos_in = query_raw + position
    pos_query = jnp.dot(pos_in, rel_square, precision=HIGH).astype(LOW)
    keys = projected[:, hq : 2 * hq].astype(LOW)
    values = projected[:, 2 * hq :].astype(LOW)
    offsets = wide_table(seq_len)
    mixed, norms = advance(
        mix(queries, keys, values, pos_query, offsets), in_flow, hid_flow
    )
    swap = Flow(seq_swap(mixed.reshape(RANKS, ROWS, hv), rank))
    norms = advance(norms, swap)
    attended = place(swap.result, SEQ, columns=True)
    r_out = w_out.shape[0]
    out_full = four[:, :r_out].reshape(HV, D)
    inputs_f = inputs_own.astype(F32)
    resid_one = inputs_f + product(attended, out_full)
    normed_flow = Flow(seq_all(layer_norm(resid_one, gain_two, bias_two).astype(LOW)))
    four = advance(four, normed_flow, in_flow)
    advance((), normed_flow)
    wholes, low = [], r_out
    for own in (w_up, w_skip, w_point):
        high = low + own.shape[0]
        wholes.append(four[:, low:high].reshape(-1, D))
        low = high
    up_full, skip_full, point_full = wholes
    normed_two = normed_flow.result
    in_part = in_flow.result.reshape(D, ff)
    hid_part = hid_flow.result.reshape(ff, D)
    pre_act = product(normed_two, in_part) + in_bias
    hidden = smooth_act(pre_act).astype(LOW)
    ff_flow = Flow(seq_sum(product(hidden, hid_part), rank))
    skip_rows = advance(skips.reshape(2 * ROWS, CS), ff_flow)
    from_skips = product(skip_rows, skip_full) + row_of["m"]
    from_skips = advance(from_skips, ff_flow)
    lift_in = (resid_one + ff_flow.result + row_of["b_hid"]).astype(LOW)
    twice = (jnp.arange(2 * ROWS)[:, None] // 2 == jnp.arange(ROWS)[None, :]).astype(LOW)
    merged = product(product(twice, lift_in).astype(LOW), up_full) + from_skips
    merged_flow = Flow(edges(merged.astype(LOW), SEQ))
    merged = advance(merged, merged_flow)
    padded = merged_flow.result.astype(F32)
    depth_out = (
        depth_full[0] * padded[:-2] + depth_full[1] * padded[1:-1] + depth_full[2] * padded[2:]
    ).astype(LOW)
    output = merged + product(depth_out, point_full) + row_of["p"]
    head_rows = output.astype(LOW)
    logits = product(head_rows, head_full) + head_bias.astype(F32)
    rate_rows = jax.nn.softplus(logits)
    count_rows = counts.reshape(2 * ROWS, TRACKS).astype(F32)
    total_rate, total_count = lax.psum(
        (jnp.sum(rate_rows, axis=0), jnp.sum(count_rows, axis=0)), SEQ
    )
    log_total = jnp.log(total_rate)
    window_terms = jnp.sum(total_count * log_total) + 0.2 * jnp.sum(
        total_rate - total_count * log_total
    )
    local_loss = -jnp.sum(count_rows * jnp.log(rate_rows)) + jnp.where(
        rank == 0, window_terms, 0.0
    )
    grad_rate = -count_rows / rate_rows + (0.2 + 0.8 * (total_count / total_rate))
    grad_rows = (grad_rate * jax.nn.sigmoid(logits)).astype(LOW)
    head_bias_part = jnp.sum(grad_rows, axis=0, dtype=F32)
    shared_flow = Flow(shared_sum(jnp.concatenate([head_bias_part, local_loss[None]])))
    head_core = Flow(core_sum(head_rows, grad_rows))
    grad_out = input_product(grad_rows, head_full).astype(LOW)
    grad_depth = input_product(grad_out, point_full).astype(LOW)
    grad_out, grad_depth = advance((grad_out, grad_depth), head_core, shared_flow)
    depth_flow = Flow(edges(grad_depth, SEQ))
    grad_out, grad_depth = advance((grad_out, grad_depth), depth_flow, shared_flow)
    head_flow = Flow(chip_sum([head_core.result], rank, window, True))
    depth_pad = depth_flow.result
    merged_low = (
        grad_out.astype(F32)
        + depth_full[0] * depth_pad[2:]
        + depth_full[1] * depth_pad[1:-1]
        + depth_full[2] * depth_pad[:-2]
    ).astype(LOW)
    lift_grad = weight_product(twice, merged_low).astype(LOW)
    grad_two = input_product(lift_grad, up_full).astype(LOW)
    grad_two, merged_low, lift_grad = advance((grad_two, merged_low, lift_grad))
    two_flow = Flow(seq_all(grad_two))
    point_core = Flow(core_sum(depth_out, grad_out))
    skip_grad = input_product(merged_low, skip_full).reshape(1, 2 * ROWS, CS)
    depth_grad = jnp.stack(
        [
            jnp.sum(grad_depth * padded[:-2], axis=0),
            jnp.sum(grad_depth * padded[1:-1], axis=0),
            jnp.sum(grad_depth * padded[2:], axis=0),
        ]
    )
    skip_grad, merged_low, grad_two, depth_grad = advance(
        (skip_grad, merged_low, grad_two, depth_grad), two_flow, point_core, shared_flow
    )
    skip_core = Flow(core_sum(skip_rows, merged_low))
    up_core = Flow(core_sum(lift_in, lift_grad))
    pbias_grad = jnp.sum(grad_out, axis=0, dtype=F32)
    mbias_grad = jnp.sum(merged_low, axis=0, dtype=F32)
    hbias_grad = jnp.sum(grad_two, axis=0, dtype=F32)
    point_flow = Flow(chip_sum([point_core.result], rank, window, False))
    pbias_grad, mbias_grad, hbias_grad = advance(
        (pbias_grad, mbias_grad, hbias_grad), two_flow, skip_core, up_core, shared_flow
    )
    up_flow = Flow(chip_sum([up_core.result], rank, window, False))
    grad_two_all = two_flow.result
    grad_hidden = input_product(grad_two_all, hid_part).astype(LOW)
    _, pull_act = jax.vjp(smooth_act, pre_act)
    grad_pre = pull_act(grad_hidden.astype(F32))[0].astype(LOW)
    pre_flow = Flow(seq_sum(input_product(grad_pre, in_part), rank))
    hid_parts = split_product(hidden, grad_two_all, WIN, ff // WINDOWS)
    in_parts = split_product(normed_two, grad_pre, WIN, D // WINDOWS)
    hid_parts, in_parts, grad_pre, skips_kept = advance(
        (hid_parts, in_parts, grad_pre, skip_core.result), pre_flow, point_flow, shared_flow
    )
    hid_flow = Flow(win_sum(*hid_parts, window))
    ibias_part = jnp.sum(grad_pre, axis=0, dtype=F32)
    ibias_part, in_parts = advance(
        (ibias_part, in_parts), pre_flow, head_flow, up_flow, point_flow
    )
    in_flow = Flow(win_sum(*in_parts, window))
    _, pull_two = jax.vjp(layer_norm, resid_one, gain_two, bias_two)
    grad_resid, gain_two_grad, bias_two_grad = pull_two(pre_flow.result)
    grad_one = (grad_two.astype(F32) + grad_resid).astype(LOW)
    grad_att = input_product(grad_one, out_full).astype(LOW)
    att_flow = Flow(
        seq_swap(
            jnp.stack([grad_att[:, t * hv : (t + 1) * hv] for t in range(RANKS)]), rank
        )
    )
    grad_one, gain_two_grad, bias_two_grad, skips_kept = advance(
        (grad_one, gain_two_grad, bias_two_grad, skips_kept), att_flow, hid_flow
    )
    out_core = Flow(core_sum(attended, grad_one))
    grad_att = place(att_flow.result, SEQ).reshape(seq_len, hv)
    query_low, pos_low, key_grad, value_grad, skips_kept = advance(
        (
            *mix_grad(queries, keys, values, pos_query, offsets, norms, grad_att),
            skips_kept,
        ),
        in_flow,
        hid_flow,
        out_core,
        up_flow,
        head_flow,
    )
    rest_flow = Flow(chip_sum([skips_kept, out_core.result], rank, window, False))
    pos_f = pos_low.astype(F32)
    pos_in_grad = lax.dot_general(
        pos_f, rel_square, (((1,), (1,)), ((), ())), precision=HIGH
    )
    query_grad = (0.125 * (query_low.astype(F32) + pos_in_grad)).astype(LOW)
    qkv_out = jnp.concatenate([query_grad, key_grad, value_grad], axis=1)
    content_part = jnp.sum(query_low, axis=0, dtype=F32)
    rel_cross = lax.dot_general(pos_f, pos_in, (((0,), (0,)), ((), ())), precision=HIGH)
    rel_rows = jnp.sum(
        jnp.where(same_head.T, rel_cross, 0.0).reshape(heads_here, BASIS, hq), axis=0
    )
    position_part = jnp.sum(pos_in_grad, axis=0)
    partial = input_product(qkv_out, qkv_part)
    centred = inputs_all.astype(F32)
    centred = centred - jnp.mean(centred, axis=-1, keepdims=True)
    scale = lax.rsqrt(jnp.mean(centred * centred, axis=-1, keepdims=True) + EPS)
    gain_one_grad = jnp.sum(partial * (centred * scale), axis=0)
    bias_one_grad = jnp.sum(partial, axis=0)
    extra = pack_grads(
        {
            "gain1": gain_one_grad,
            "bias1": bias_one_grad,
            "gain2": gain_two_grad,
            "bias2": bias_two_grad,
            "b_hid": hbias_grad,
            "m": mbias_grad,
            "p": pbias_grad,
            "d0": depth_grad[0],
            "d1": depth_grad[1],
            "d2": depth_grad[2],
        },
        ibias_part,
        content_part,
        position_part,
        rel_rows,
    ).astype(LOW)
    qkv_kept, qkv_sent = split_product(normed, qkv_out, WIN, D // WINDOWS)
    y = window % 2
    extra = extra.reshape(WINDOWS // 2, 2, RANKS, EXTRA, ROOM)

    def with_extra(grads, index):
        grads = grads.reshape(WINDOWS // 2, RANKS, -1, ROOM)
        short = lax.dynamic_index_in_dim(extra, index, 1, keepdims=False)
        return jnp.concatenate([grads, short], axis=2).reshape(WINDOWS // 2, -1, ROOM)

    qkv_kept, qkv_sent = advance(
        (with_extra(qkv_kept, y), with_extra(qkv_sent, 1 - y)),
        in_flow,
        hid_flow,
        point_flow,
        up_flow,
    )
    qkv_flow = Flow(win_sum(qkv_kept, qkv_sent, window))
    one_flow = Flow(seq_sum(partial, rank))
    advance((), one_flow, in_flow, head_flow, rest_flow)
    in_back = in_flow.result.astype(LOW).reshape(RANKS, -1, ff)
    in_back = advance(in_back, one_flow, qkv_flow, point_flow, up_flow)
    in_back = Flow(seq_swap_two(in_back, rank))
    grad_normed = one_flow.result
    _, pull_one = jax.vjp(lambda rows: layer_norm(rows, gain_one, bias_one), inputs_f)
    (grad_norm_in,) = pull_one(grad_normed)
    grad_inputs = (grad_one.astype(F32) + grad_norm_in).reshape(1, ROWS, D)
    advance((), qkv_flow, head_flow, in_back, rest_flow)
    advance((), qkv_flow, in_back, rest_flow)
    qkv_flow = Flow(seq_swap(qkv_flow.result.astype(LOW).reshape(RANKS, -1, ROOM), rank))
    advance((), qkv_flow, rest_flow)
    wq_grad, wk_grad, wv_grad, shorts, rel_grad = finish(qkv_flow.result, hq, hv)
    sums = {name: shorts[0, low:high] for name, (low, high) in SHORT.items()}
    in_grad = undeal(in_back.result, WINDOWS)
    (point_grad,), (up_grad,) = point_flow.result, up_flow.result
    skip_weight_grad, out_grad = rest_flow.result
    (head_grad,) = head_flow.result
    hid_grad = hid_flow.result
    loss_total, head_bias_grad = shared_flow.result[-1], shared_flow.result[:-1]
    loss_mean = loss_total / (WINDOWS * 2 * seq_len * TRACKS)
    return (
        loss_mean,
        head_rows.reshape(1, 2 * ROWS, D),
        grad_inputs,
        skip_grad,
        sums["gain1"],
        sums["bias1"],
        wq_grad,
        wk_grad,
        wv_grad,
        rel_grad,
        sums["con"],
        sums["pos"],
        out_grad,
        sums["gain2"],
        sums["bias2"],
        in_grad,
        sums["b_in"],
        hid_grad,
        sums["b_hid"],
        up_grad,
        skip_weight_grad,
        sums["m"],
        jnp.stack([sums["d0"], sums["d1"], sums["d2"]]),
        point_grad,
        sums["p"],
        head_grad,
        head_bias_grad,
    )


def general_body(
    inputs,
    skips,
    counts,
    ln1_gain,
    ln1_bias,
    w_query,
    w_key,
    w_value,
    w_rel,
    content_bias,
    position_bias,
    w_out,
    ln2_gain,
    ln2_bias,
    w_in,
    b_in,
    w_hid,
    b_hid,
    w_up,
    w_skip,
    m_bias,
    w_depth,
    w_point,
    p_bias,
    w_head,
    head_bias,
):
    seq_count = lax.axis_size(SEQ)
    seq_len = TOK_SEQ * seq_count
    first_pos = lax.axis_index(SEQ) * TOK_SEQ
    row_count = SEQS_DEV * TOK_SEQ
    blk_len = 512
    blk_count = seq_len // blk_len
    blk_steps = jnp.arange(blk_count, dtype=jnp.int32)
    mixer_full = (
        lax.all_gather(ln1_gain, BOTH, axis=0, tiled=True),
        lax.all_gather(ln1_bias, BOTH, axis=0, tiled=True),
        lax.all_gather(w_query, BOTH, axis=0, tiled=True),
        lax.all_gather(w_key, BOTH, axis=0, tiled=True),
        lax.all_gather(w_value, BOTH, axis=0, tiled=True),
        lax.all_gather(w_rel, BOTH, axis=1, tiled=True),
        lax.all_gather(content_bias, BOTH, axis=0, tiled=True),
        lax.all_gather(position_bias, BOTH, axis=0, tiled=True),
        lax.all_gather(w_out, BOTH, axis=0, tiled=True),
    )
    tail_full = (
        lax.all_gather(ln2_gain, BOTH, axis=0, tiled=True),
        lax.all_gather(ln2_bias, BOTH, axis=0, tiled=True),
        lax.all_gather(w_in, BOTH, axis=0, tiled=True),
        lax.all_gather(b_in, BOTH, axis=0, tiled=True),
        lax.all_gather(w_hid, BOTH, axis=0, tiled=True),
        lax.all_gather(b_hid, BOTH, axis=0, tiled=True),
        lax.all_gather(w_up, BOTH, axis=0, tiled=True),
        lax.all_gather(w_skip, BOTH, axis=0, tiled=True),
        lax.all_gather(m_bias, BOTH, axis=0, tiled=True),
        lax.all_gather(w_depth, BOTH, axis=1, tiled=True),
        lax.all_gather(w_point, BOTH, axis=0, tiled=True),
        lax.all_gather(p_bias, BOTH, axis=0, tiled=True),
        lax.all_gather(w_head, BOTH, axis=0, tiled=True),
    )
    gain_one = mixer_full[0].astype(jnp.float32)
    bias_one = mixer_full[1].astype(jnp.float32)
    query_full = mixer_full[2]
    key_full = mixer_full[3]
    value_full = mixer_full[4]
    rel_full = mixer_full[5].astype(jnp.float32).reshape(BASIS, HEADS, KEY)
    content_full = mixer_full[6].astype(jnp.float32)
    position_full = mixer_full[7].astype(jnp.float32)
    out_full = mixer_full[8]
    gain_two = tail_full[0].astype(jnp.float32)
    bias_two = tail_full[1].astype(jnp.float32)
    in_full = tail_full[2]
    in_bias = tail_full[3].astype(jnp.float32)
    hid_full = tail_full[4]
    hid_bias = tail_full[5].astype(jnp.float32)
    up_full = tail_full[6]
    skip_full = tail_full[7]
    merge_bias = tail_full[8].astype(jnp.float32)
    depth_full = tail_full[9].astype(jnp.float32)
    point_full = tail_full[10]
    point_bias = tail_full[11].astype(jnp.float32)
    head_full = tail_full[12]
    inputs_f = inputs.astype(jnp.float32).reshape(row_count, D)
    normed = layer_norm(inputs_f, gain_one, bias_one).astype(jnp.bfloat16)
    query_raw = product(normed, query_full) * 0.125
    queries = (query_raw + content_full).astype(jnp.bfloat16).reshape(SEQS_DEV, TOK_SEQ, HEADS, KEY)
    pos_in = (query_raw + position_full).reshape(row_count, HEADS, KEY)
    pos_query = (
        jnp.einsum("lhk,bhk->lhb", pos_in, rel_full, precision=HIGH)
        .astype(jnp.bfloat16)
        .reshape(SEQS_DEV, TOK_SEQ, HEADS, BASIS)
    )
    key_rows = product(normed, key_full).astype(jnp.bfloat16).reshape(SEQS_DEV, TOK_SEQ, HK)
    values = product(normed, value_full).astype(jnp.bfloat16).reshape(SEQS_DEV, TOK_SEQ, HV)
    keys_all, values_all = (
        lax.all_gather(key_rows, SEQ, axis=1, tiled=True),
        lax.all_gather(values, SEQ, axis=1, tiled=True),
    )

    def key_block(whole_rows, blk_index):
        return lax.dynamic_slice_in_dim(whole_rows, blk_index * blk_len, blk_len, 1)

    def value_block(blk_index):
        return key_block(values_all, blk_index).reshape(SEQS_DEV, blk_len, HEADS, VAL)

    def scores_at(blk_index):
        return score_block(
            queries,
            pos_query,
            key_block(keys_all, blk_index),
            first_pos,
            blk_index * blk_len,
            seq_len,
        )

    def max_step(state_pair, blk_index):
        row_max, row_sum = state_pair
        scores, basis_grid = scores_at(blk_index)
        new_max = jnp.maximum(row_max, jnp.max(scores, axis=-1))
        row_sum = row_sum * jnp.exp(row_max - new_max) + jnp.sum(
            jnp.exp(scores - new_max[..., None]), axis=-1
        )
        return ((new_max, row_sum), None)

    start_max = jnp.full((SEQS_DEV, HEADS, TOK_SEQ), -jnp.inf, jnp.float32)
    (row_max, row_sum), _ = lax.scan(max_step, (start_max, jnp.zeros_like(start_max)), blk_steps)
    log_norm = row_max + jnp.log(row_sum)

    def mix_step(mixed_sum, blk_index):
        scores, basis_grid = scores_at(blk_index)
        weights = jnp.exp(scores - log_norm[..., None]).astype(jnp.bfloat16)
        mixed_sum = mixed_sum + jnp.einsum(
            "shnc,schv->snhv", weights, value_block(blk_index), preferred_element_type=jnp.float32
        )
        return (mixed_sum, None)

    mixed_sum, _ = lax.scan(
        mix_step, jnp.zeros((SEQS_DEV, TOK_SEQ, HEADS, VAL), jnp.float32), blk_steps
    )
    attended = mixed_sum.reshape(row_count, HV).astype(jnp.bfloat16)
    resid_one = inputs_f + product(attended, out_full)
    normed_two = layer_norm(resid_one, gain_two, bias_two).astype(jnp.bfloat16)
    pre_act = product(normed_two, in_full) + in_bias
    hidden = smooth_act(pre_act).astype(jnp.bfloat16)
    lift_in = (resid_one + product(hidden, hid_full) + hid_bias).astype(jnp.bfloat16)
    lifted = product(lift_in, up_full).reshape(SEQS_DEV, TOK_SEQ, D)
    skip_rows = skips.reshape(2 * row_count, CS)
    merged = (
        jnp.repeat(lifted, 2, axis=1)
        + product(skip_rows, skip_full).reshape(SEQS_DEV, 2 * TOK_SEQ, D)
        + merge_bias
    )
    padded = with_halo(merged.astype(jnp.bfloat16), ((SEQ, 1),), 1).astype(merged.dtype)
    depth_out = (
        depth_full[0] * padded[:, :-2]
        + depth_full[1] * padded[:, 1:-1]
        + depth_full[2] * padded[:, 2:]
    ).astype(jnp.bfloat16)
    output = (
        merged
        + product(depth_out.reshape(2 * row_count, D), point_full).reshape(SEQS_DEV, 2 * TOK_SEQ, D)
        + point_bias
    )
    head_in = output.astype(jnp.bfloat16)
    head_rows = head_in.reshape(2 * row_count, D)
    logits = (product(head_rows, head_full) + head_bias.astype(jnp.float32)).reshape(
        SEQS_DEV, 2 * TOK_SEQ, TRACKS
    )
    rate_rows = jax.nn.softplus(logits)
    count_rows = counts.astype(jnp.float32)
    part_rate = jnp.sum(rate_rows, axis=1)
    part_count = jnp.sum(count_rows, axis=1)
    total_rate, total_count = lax.psum((part_rate, part_count), SEQ)
    log_total = jnp.log(total_rate)
    window_terms = jnp.sum(total_count * log_total) + 0.2 * jnp.sum(
        total_rate - total_count * log_total
    )
    local_loss = -jnp.sum(count_rows * jnp.log(rate_rows)) + jnp.where(
        lax.axis_index(SEQ) == 0, window_terms, 0.0
    )
    count_ratio = total_count / total_rate
    grad_rate = -count_rows / rate_rows + (0.2 + 0.8 * count_ratio)[:, None, :]
    grad_logit = (grad_rate * jax.nn.sigmoid(logits)).astype(jnp.bfloat16)
    bias_part = jnp.sum(grad_logit, axis=(0, 1), dtype=jnp.float32)
    loss_total, head_bias_grad = lax.psum((local_loss, bias_part), BOTH)
    loss_mean = loss_total / (SEQS_DEV * lax.axis_size(WIN) * 2 * seq_len * TRACKS)
    grad_rows = grad_logit.reshape(2 * row_count, TRACKS)
    head_grad = weight_product(head_rows, grad_rows)
    grad_out = input_product(grad_rows, head_full).astype(jnp.bfloat16)
    point_grad = weight_product(depth_out.reshape(2 * row_count, D), grad_out)
    pbias_grad = jnp.sum(grad_out, axis=0, dtype=jnp.float32)
    grad_depth = (
        input_product(grad_out, point_full).astype(jnp.bfloat16).reshape(SEQS_DEV, 2 * TOK_SEQ, D)
    )
    depth_grad = jnp.stack(
        [
            jnp.sum(grad_depth * padded[:, :-2], axis=(0, 1)),
            jnp.sum(grad_depth * padded[:, 1:-1], axis=(0, 1)),
            jnp.sum(grad_depth * padded[:, 2:], axis=(0, 1)),
        ]
    )
    depth_pad = with_halo(grad_depth, ((SEQ, 1),), 1)
    grad_merged = (
        grad_out.reshape(SEQS_DEV, 2 * TOK_SEQ, D).astype(jnp.float32)
        + depth_full[0] * depth_pad[:, 2:]
        + depth_full[1] * depth_pad[:, 1:-1]
        + depth_full[2] * depth_pad[:, :-2]
    )
    merged_low = grad_merged.astype(jnp.bfloat16)
    merged_rows = merged_low.reshape(2 * row_count, D)
    skip_weight_grad = weight_product(skip_rows, merged_rows)
    skip_grad = input_product(merged_rows, skip_full).reshape(SEQS_DEV, 2 * TOK_SEQ, CS)
    mbias_grad = jnp.sum(merged_rows, axis=0, dtype=jnp.float32)
    lift_grad = (
        jnp.sum(merged_low.reshape(SEQS_DEV, TOK_SEQ, 2, D), axis=2, dtype=jnp.float32)
        .reshape(row_count, D)
        .astype(jnp.bfloat16)
    )
    up_grad = weight_product(lift_in, lift_grad)
    grad_two = input_product(lift_grad, up_full).astype(jnp.bfloat16)
    hid_grad = weight_product(hidden, grad_two)
    hbias_grad = jnp.sum(grad_two, axis=0, dtype=jnp.float32)
    grad_hidden = input_product(grad_two, hid_full).astype(jnp.bfloat16)
    _, pull_act = jax.vjp(smooth_act, pre_act)
    grad_pre = pull_act(grad_hidden.astype(jnp.float32))[0].astype(jnp.bfloat16)
    in_grad = weight_product(normed_two, grad_pre)
    ibias_grad = jnp.sum(grad_pre, axis=0, dtype=jnp.float32)
    _, pull_two = jax.vjp(layer_norm, resid_one, gain_two, bias_two)
    grad_resid, gain_two_grad, bias_two_grad = pull_two(input_product(grad_pre, in_full))
    grad_one = (grad_two.astype(jnp.float32) + grad_resid).astype(jnp.bfloat16)
    out_grad = weight_product(attended, grad_one)
    grad_att = (
        input_product(grad_one, out_full)
        .astype(jnp.bfloat16)
        .reshape(SEQS_DEV, TOK_SEQ, HEADS, VAL)
    )

    def grad_parts(blk_index):
        key_blk = key_block(keys_all, blk_index)
        scores, basis_grid = score_block(
            queries, pos_query, key_blk, first_pos, blk_index * blk_len, seq_len
        )
        soft_probs = jnp.exp(scores - log_norm[..., None])
        prob_grad = jnp.einsum(
            "snhv,schv->shnc", grad_att, value_block(blk_index), preferred_element_type=jnp.float32
        )
        return (key_blk, basis_grid, soft_probs, prob_grad)

    def delta_step(delta_sum, blk_index):
        key_blk, basis_grid, soft_probs, prob_grad = grad_parts(blk_index)
        return (delta_sum + jnp.sum(soft_probs * prob_grad, axis=-1), None)

    row_delta, _ = lax.scan(
        delta_step, jnp.zeros((SEQS_DEV, HEADS, TOK_SEQ), jnp.float32), blk_steps
    )

    def query_terms(state_pair, blk_index):
        key_blk, basis_grid, soft_probs, prob_grad = grad_parts(blk_index)
        score_grad = (soft_probs * (prob_grad - row_delta[..., None])).astype(jnp.bfloat16)
        key_heads = key_blk.reshape(SEQS_DEV, blk_len, HEADS, KEY)
        query_acc = state_pair[0] + jnp.einsum(
            "shnc,schk->snhk", score_grad, key_heads, preferred_element_type=jnp.float32
        )
        pos_acc = state_pair[1] + jnp.einsum(
            "shnc,ncb->snhb", score_grad, basis_grid, preferred_element_type=jnp.float32
        )
        return ((query_acc, pos_acc), score_grad, soft_probs)

    query_zero = jnp.zeros((SEQS_DEV, TOK_SEQ, HEADS, KEY), jnp.float32)
    pos_zero = jnp.zeros((SEQS_DEV, TOK_SEQ, HEADS, BASIS), jnp.float32)

    def sum_step(state_four, blk_index):
        pair_next, score_grad, soft_probs = query_terms((state_four[0], state_four[1]), blk_index)
        key_part = jnp.einsum(
            "shnc,snhk->schk", score_grad, queries, preferred_element_type=jnp.float32
        ).reshape(SEQS_DEV, blk_len, HK)
        value_part = jnp.einsum(
            "shnc,snhv->schv",
            soft_probs.astype(jnp.bfloat16),
            grad_att,
            preferred_element_type=jnp.float32,
        ).reshape(SEQS_DEV, blk_len, HV)
        key_acc = lax.dynamic_update_slice_in_dim(state_four[2], key_part, blk_index * blk_len, 1)
        value_acc = lax.dynamic_update_slice_in_dim(
            state_four[3], value_part, blk_index * blk_len, 1
        )
        return ((pair_next[0], pair_next[1], key_acc, value_acc), None)

    start_four = (
        query_zero,
        pos_zero,
        jnp.zeros((SEQS_DEV, seq_len, HK), jnp.float32),
        jnp.zeros((SEQS_DEV, seq_len, HV), jnp.float32),
    )
    (query_acc, pos_acc, key_terms_all, value_terms_all), _ = lax.scan(
        sum_step, start_four, blk_steps
    )
    key_sum, value_sum = (
        lax.psum_scatter(
            key_terms_all.astype(jnp.bfloat16), SEQ, scatter_dimension=1, tiled=True
        ).astype(jnp.float32),
        lax.psum_scatter(
            value_terms_all.astype(jnp.bfloat16), SEQ, scatter_dimension=1, tiled=True
        ).astype(jnp.float32),
    )
    key_grad = key_sum.reshape(row_count, HK).astype(jnp.bfloat16)
    value_grad = value_sum.reshape(row_count, HV).astype(jnp.bfloat16)
    query_low = query_acc.astype(jnp.bfloat16).reshape(row_count, HK)
    content_grad = jnp.sum(query_low, axis=0, dtype=jnp.float32)
    pos_low = pos_acc.astype(jnp.bfloat16).reshape(row_count, HEADS, BASIS).astype(jnp.float32)
    pos_in_grad = jnp.einsum("lhb,bhk->lhk", pos_low, rel_full, precision=HIGH)
    rel_grad = jnp.einsum("lhb,lhk->bhk", pos_low, pos_in, precision=HIGH).reshape(BASIS, HK)
    position_grad = jnp.sum(pos_in_grad, axis=0).reshape(HK)
    query_grad = (
        0.125 * (query_low.astype(jnp.float32) + pos_in_grad.reshape(row_count, HK))
    ).astype(jnp.bfloat16)
    wq_grad = weight_product(normed, query_grad)
    wk_grad = weight_product(normed, key_grad)
    wv_grad = weight_product(normed, value_grad)
    grad_normed = (
        input_product(query_grad, query_full)
        + input_product(key_grad, key_full)
        + input_product(value_grad, value_full)
    )
    _, pull_one = jax.vjp(layer_norm, inputs_f, gain_one, bias_one)
    grad_norm_in, gain_one_grad, bias_one_grad = pull_one(grad_normed)
    grad_inputs = (grad_one.astype(jnp.float32) + grad_norm_in).reshape(SEQS_DEV, TOK_SEQ, D)
    mixer_grads = (
        lax.psum_scatter(gain_one_grad, BOTH, scatter_dimension=0, tiled=True),
        lax.psum_scatter(bias_one_grad, BOTH, scatter_dimension=0, tiled=True),
        lax.psum_scatter(wq_grad, BOTH, scatter_dimension=0, tiled=True),
        lax.psum_scatter(wk_grad, BOTH, scatter_dimension=0, tiled=True),
        lax.psum_scatter(wv_grad, BOTH, scatter_dimension=0, tiled=True),
        lax.psum_scatter(rel_grad, BOTH, scatter_dimension=1, tiled=True),
        lax.psum_scatter(content_grad, BOTH, scatter_dimension=0, tiled=True),
        lax.psum_scatter(position_grad, BOTH, scatter_dimension=0, tiled=True),
        lax.psum_scatter(out_grad, BOTH, scatter_dimension=0, tiled=True),
    )
    tail_grads = (
        lax.psum_scatter(gain_two_grad, BOTH, scatter_dimension=0, tiled=True),
        lax.psum_scatter(bias_two_grad, BOTH, scatter_dimension=0, tiled=True),
        lax.psum_scatter(in_grad, BOTH, scatter_dimension=0, tiled=True),
        lax.psum_scatter(ibias_grad, BOTH, scatter_dimension=0, tiled=True),
        lax.psum_scatter(hid_grad, BOTH, scatter_dimension=0, tiled=True),
        lax.psum_scatter(hbias_grad, BOTH, scatter_dimension=0, tiled=True),
        lax.psum_scatter(up_grad, BOTH, scatter_dimension=0, tiled=True),
        lax.psum_scatter(skip_weight_grad, BOTH, scatter_dimension=0, tiled=True),
        lax.psum_scatter(mbias_grad, BOTH, scatter_dimension=0, tiled=True),
        lax.psum_scatter(depth_grad, BOTH, scatter_dimension=1, tiled=True),
        lax.psum_scatter(point_grad, BOTH, scatter_dimension=0, tiled=True),
        lax.psum_scatter(pbias_grad, BOTH, scatter_dimension=0, tiled=True),
        lax.psum_scatter(head_grad, BOTH, scatter_dimension=0, tiled=True),
    )
    return (
        (loss_mean, head_in, grad_inputs, skip_grad)
        + tuple(mixer_grads)
        + tuple(tail_grads)
        + (head_bias_grad,)
    )


SPLIT, ROWED, TILED = P(BOTH), P(BOTH, None), P(WIN, SEQ, None)


def solution(mesh):
    paired = mesh.shape[WIN] == 8 and mesh.shape[SEQ] == 4
    return jax.shard_map(
        split_body if paired else general_body,
        mesh=mesh,
        in_specs=(
            TILED,
            TILED,
            TILED,
            SPLIT,
            SPLIT,
            ROWED,
            ROWED,
            ROWED,
            P(None, BOTH),
            SPLIT,
            SPLIT,
            ROWED,
            SPLIT,
            SPLIT,
            ROWED,
            SPLIT,
            ROWED,
            SPLIT,
            ROWED,
            ROWED,
            SPLIT,
            P(None, BOTH),
            ROWED,
            SPLIT,
            ROWED,
            P(),
        ),
        out_specs=(
            P(),
            TILED,
            TILED,
            TILED,
            SPLIT,
            SPLIT,
            ROWED,
            ROWED,
            ROWED,
            P(None, BOTH),
            SPLIT,
            SPLIT,
            ROWED,
            SPLIT,
            SPLIT,
            ROWED,
            SPLIT,
            ROWED,
            SPLIT,
            ROWED,
            ROWED,
            SPLIT,
            P(None, BOTH),
            ROWED,
            SPLIT,
            ROWED,
            P(),
        ),
        check_vma=False,
    )
```

```python
import functools
import math

import jax
import jax.numpy as jnp
from jax import lax
from jax.experimental import pallas as pl
from jax.experimental.pallas import tpu as pltpu
from jax.sharding import PartitionSpec as P

D = 1536
HEADS = 8
KEY = 64
VAL = 192
BASIS = 32
CS = 1280
TRACKS = 2608
TOK_SEQ = 256
SEQS_DEV = 1
HK = 512
HV = 1536


WIN, SEQ = "win", "seq"
BOTH = (WIN, SEQ)
EPS = 1e-05
HIGH = lax.Precision.HIGHEST


def with_halo(cells, sides, width):
    for axis, dim in sides:
        count = lax.axis_size(axis)
        ends = count - 1
        head = lax.slice_in_dim(cells, 0, width, axis=dim)
        tail = lax.slice_in_dim(cells, cells.shape[dim] - width, cells.shape[dim], axis=dim)
        cells = jnp.concatenate(
            [
                lax.ppermute(tail, axis, [(i, (i + 1) % count) for i in range(ends)]),
                cells,
                lax.ppermute(head, axis, [((i + 1) % count, i) for i in range(ends)]),
            ],
            axis=dim,
        )
    return cells


def basis_table(offsets, seq_len, basis_count):
    halves = basis_count // 2
    ramped = jnp.arange(halves, dtype=jnp.int32).astype(jnp.float32) / (halves - 1)
    half_life = 3.0 * jnp.exp(ramped * math.log(seq_len / 3.0))
    distance = jnp.abs(offsets)[..., None]
    decays = jnp.exp(-math.log(2.0) * distance / half_life)
    return jnp.concatenate([decays, jnp.sign(offsets)[..., None] * decays], axis=-1)


def layer_norm(values, gain_row, bias_row):
    centred = values - jnp.mean(values, axis=-1, keepdims=True)
    spread = jnp.mean(centred * centred, axis=-1, keepdims=True)
    return centred * lax.rsqrt(spread + EPS) * gain_row + bias_row


def smooth_act(values):
    return jax.nn.gelu(values, approximate=True)


def product(first_arg, second_arg):
    return jnp.dot(first_arg, second_arg, preferred_element_type=jnp.float32)


def weight_product(first_arg, second_arg):
    return lax.dot_general(
        first_arg, second_arg, (((0,), (0,)), ((), ())), preferred_element_type=jnp.float32
    )


def input_product(first_arg, second_arg):
    return lax.dot_general(
        first_arg, second_arg, (((1,), (1,)), ((), ())), preferred_element_type=jnp.float32
    )


def score_block(query_blk, pos_blk, key_blk, query_first, key_first, seq_len):
    row_pos = query_first + jnp.arange(query_blk.shape[1], dtype=jnp.int32)
    col_pos = key_first + jnp.arange(key_blk.shape[1], dtype=jnp.int32)
    offsets = (row_pos[:, None] - col_pos[None, :]).astype(jnp.float32)
    basis_grid = basis_table(offsets, seq_len, BASIS).astype(jnp.bfloat16)
    key_heads = key_blk.reshape(key_blk.shape[0], key_blk.shape[1], HEADS, KEY)
    content = jnp.einsum(
        "snhk,schk->shnc", query_blk, key_heads, preferred_element_type=jnp.float32
    )
    position = jnp.einsum("snhb,ncb->shnc", pos_blk, basis_grid, preferred_element_type=jnp.float32)
    return (content + position, basis_grid)


F32 = jnp.float32
LOW = jnp.bfloat16
ROWS = 256
FF = 3072
RANKS = 4
WINDOWS = 8


def wide_table(seq_len):
    offsets = (seq_len - 1 - jnp.arange(2 * seq_len, dtype=jnp.int32)).astype(F32)
    return basis_table(offsets, seq_len, BASIS).astype(LOW).T


def offset_window(table_ref, keys):
    start = keys - ROWS - pl.program_id(0) * ROWS
    return table_ref[:, pl.ds(pl.multiple_of(start, 128), keys + ROWS)]


def row_scores(query, key, pos_query, window):
    keys = key.shape[0]
    wide = product(pos_query, window)
    lined = pltpu.roll(wide, keys + 1, 1, stride=1, stride_axis=0)
    return input_product(query, key) + lined[:, :keys]


def head_columns(head):
    return (
        slice(head * KEY, (head + 1) * KEY),
        slice(head * VAL, (head + 1) * VAL),
        slice(head * BASIS, (head + 1) * BASIS),
    )


def mix_kernel(heads, q_ref, k_ref, v_ref, pos_ref, table_ref, out_ref, norm_ref):
    window = offset_window(table_ref, k_ref.shape[0])
    for head in range(heads):
        ks, vs, bs = head_columns(head)
        scores = row_scores(q_ref[:, ks], k_ref[:, ks], pos_ref[:, bs], window)
        top = jnp.max(scores, axis=1, keepdims=True)
        powers = jnp.exp(scores - top)
        total = jnp.sum(powers, axis=1, keepdims=True)
        weights = (powers * (1.0 / total)).astype(LOW)
        out_ref[:, vs] = product(weights, v_ref[:, vs]).astype(LOW)
        norm_ref[:, head : head + 1] = top + jnp.log(total)


def mix_grad_kernel(
    heads,
    q_ref,
    k_ref,
    v_ref,
    pos_ref,
    table_ref,
    norm_ref,
    ga_ref,
    dq_ref,
    dpos_ref,
    dk_ref,
    dv_ref,
    dk_sum,
    dv_sum,
):
    step = pl.program_id(0)
    keys = k_ref.shape[0]
    window = offset_window(table_ref, keys)
    down = lax.broadcasted_iota(jnp.int32, (ROWS, ROWS), 0)
    across = lax.broadcasted_iota(jnp.int32, (ROWS, ROWS), 1)
    flip = (down + across == ROWS - 1).astype(LOW)

    @pl.when(step == 0)
    def _():
        dk_sum[...] = jnp.zeros_like(dk_sum)
        dv_sum[...] = jnp.zeros_like(dv_sum)

    for head in range(heads):
        ks, vs, bs = head_columns(head)
        query, key, value, grad = q_ref[:, ks], k_ref[:, ks], v_ref[:, vs], ga_ref[:, vs]
        scores = row_scores(query, key, pos_ref[:, bs], window)
        probs = jnp.exp(scores - norm_ref[:, head : head + 1])
        dprob = input_product(grad, value)
        delta = jnp.sum(probs * dprob, axis=1, keepdims=True)
        dscore = (probs * (dprob - delta)).astype(LOW)
        dq_ref[:, ks] = product(dscore, key).astype(LOW)
        dk_sum[:, ks] += weight_product(dscore, query)
        dv_sum[:, vs] += weight_product(probs.astype(LOW), grad)
        wide = jnp.concatenate([product(flip, dscore), jnp.zeros((ROWS, ROWS), F32)], axis=1)
        lined = pltpu.roll(wide, 0, 1, stride=1, stride_axis=0).astype(LOW)
        turned = input_product(lined, window).astype(LOW)
        dpos_ref[:, bs] = product(flip, turned).astype(LOW)

    @pl.when(step == pl.num_programs(0) - 1)
    def _():
        dk_ref[...] = dk_sum[...].astype(LOW)
        dv_ref[...] = dv_sum[...].astype(LOW)


def row_spec(array):
    return pl.BlockSpec((ROWS, array.shape[1]), lambda i: (i, 0))


def whole_spec(array):
    return pl.BlockSpec(array.shape, lambda i: (0, 0))


def mix(query, key, value, pos_query, table):
    rows, keys = query.shape[0], key.shape[0]
    heads = key.shape[1] // KEY
    norm = jax.ShapeDtypeStruct((rows, heads), F32)
    out = jax.ShapeDtypeStruct((rows, value.shape[1]), LOW)
    return pl.pallas_call(
        functools.partial(mix_kernel, heads),
        grid=(rows // ROWS,),
        in_specs=[
            row_spec(query),
            whole_spec(key),
            whole_spec(value),
            row_spec(pos_query),
            whole_spec(table),
        ],
        out_specs=[row_spec(out), row_spec(norm)],
        out_shape=[out, norm],
        compiler_params=pltpu.CompilerParams(vmem_limit_bytes=40 * 2**20),
        cost_estimate=pl.CostEstimate(
            flops=10**10, transcendentals=rows * keys * heads, bytes_accessed=4 * 2**20
        ),
    )(query, key, value, pos_query, table)


def mix_grad(query, key, value, pos_query, table, norm, grad):
    rows, keys = query.shape[0], key.shape[0]
    heads = key.shape[1] // KEY

    def like(array):
        return jax.ShapeDtypeStruct(array.shape, LOW)

    return pl.pallas_call(
        functools.partial(mix_grad_kernel, heads),
        grid=(rows // ROWS,),
        in_specs=[
            row_spec(query),
            whole_spec(key),
            whole_spec(value),
            row_spec(pos_query),
            whole_spec(table),
            row_spec(norm),
            row_spec(grad),
        ],
        out_specs=[row_spec(query), row_spec(pos_query), whole_spec(key), whole_spec(value)],
        out_shape=[like(query), like(pos_query), like(key), like(value)],
        scratch_shapes=[pltpu.VMEM(key.shape, F32), pltpu.VMEM(value.shape, F32)],
        compiler_params=pltpu.CompilerParams(vmem_limit_bytes=40 * 2**20),
        cost_estimate=pl.CostEstimate(
            flops=15 * 10**9, transcendentals=rows * keys * heads, bytes_accessed=6 * 2**20
        ),
    )(query, key, value, pos_query, table, norm, grad)


def trade(block, axis, bits):
    count = lax.axis_size(axis)
    return lax.ppermute(block, axis, [(i, i ^ bits) for i in range(count)])


def in_order(pieces, index):
    pieces = list(pieces)
    bit = 1
    while bit < len(pieces):
        odd = (index & bit) != 0
        pieces = [jnp.where(odd, pieces[k ^ bit], pieces[k]) for k in range(len(pieces))]
        bit *= 2
    return pieces


def place_kernel(axis, shift, inner, columns, *refs):
    index = lax.axis_index(axis)
    index = index // shift if shift > 1 else index
    count = len(refs) - 1
    out_ref = refs[count]
    for k in range(count):
        to = (index % count) ^ k
        if columns:
            width = refs[k].shape[1]
            out_ref[:, pl.ds(pl.multiple_of(to * width, 128), width)] = refs[k][...]
        elif inner:
            for outer in range(inner):
                out_ref[outer, to] = refs[k][outer]
        else:
            out_ref[to] = refs[k][...]


def place(pieces, axis, shift=1, inner=0, columns=False):
    count, shape = len(pieces), pieces[0].shape
    if columns:
        shape = (shape[0], count * shape[1])
    elif inner:
        shape = (inner, count) + shape[1:]
    else:
        shape = (count,) + shape
    return pl.pallas_call(
        functools.partial(place_kernel, axis, shift, inner, columns),
        out_shape=jax.ShapeDtypeStruct(shape, pieces[0].dtype),
        compiler_params=pltpu.CompilerParams(vmem_limit_bytes=24 * 2**20),
        cost_estimate=pl.CostEstimate(flops=0, transcendentals=0, bytes_accessed=1024),
    )(*pieces)


def pick(blocks, index):
    return lax.dynamic_index_in_dim(blocks, index, 0, keepdims=False)


tie = lax.optimization_barrier


class Flow:
    def __init__(self, stages):
        self.stages, self.result = stages, None
        self.pending = next(stages)

    def step(self, arrived):
        try:
            self.pending = self.stages.send(arrived)
        except StopIteration as last:
            self.pending, self.result = (), last.value


def advance(values, *flows):
    values, arrived = tie((tie(values), [flow.pending for flow in flows]))
    for flow, rows in zip(flows, arrived):
        flow.step(rows)
    return values


def seq_all(rows):
    near, far = yield trade(rows, SEQ, 1), trade(rows, SEQ, 2)
    last = yield trade(far, SEQ, 1)
    return place([rows, near, far, last], SEQ).reshape(RANKS * rows.shape[0], rows.shape[1])


def seq_sum(partial, rank):
    blocks = partial.reshape(RANKS, ROWS, partial.shape[1])
    got = yield trade(jnp.stack([pick(blocks, rank ^ 1), pick(blocks, rank ^ 3)]), SEQ, 1)
    last = yield trade(plus(pick(blocks, rank ^ 2), got[1]), SEQ, 2)
    return pick(blocks, rank).astype(F32) + got[0].astype(F32) + last.astype(F32)


def seq_swap(blocks, rank):
    got = yield [trade(pick(blocks, rank ^ k), SEQ, k) for k in range(1, RANKS)]
    return [pick(blocks, rank)] + got


def seq_swap_two(blocks, rank):
    far = yield trade(jnp.stack([pick(blocks, rank ^ 2), pick(blocks, rank ^ 3)]), SEQ, 2)
    near = yield trade(jnp.stack([pick(blocks, rank ^ 1), far[1]]), SEQ, 1)
    return [pick(blocks, rank), near[0], far[0], near[1]]


def deal_kernel(parts, whole_ref, dealt_ref):
    width = whole_ref.shape[1] // (RANKS * parts)
    for t in range(RANKS):
        for p in range(parts):
            first = (p * RANKS + t) * width
            dealt_ref[t, :, p * width : (p + 1) * width] = whole_ref[:, first : first + width]


def deal(array, parts):
    rows, columns = array.shape
    return pl.pallas_call(
        functools.partial(deal_kernel, parts),
        out_shape=jax.ShapeDtypeStruct((RANKS, rows, columns // RANKS), array.dtype),
    )(array)


def undeal_kernel(parts, *refs):
    rank = lax.axis_index(SEQ)
    width = refs[0].shape[1] // parts
    pieces = [ref[...].astype(F32) for ref in refs[:RANKS]]
    for bit in (1, 2):
        odd = (rank & bit) != 0
        pieces = [jnp.where(odd, pieces[k ^ bit], pieces[k]) for k in range(RANKS)]
    for t in range(RANKS):
        for p in range(parts):
            first = (p * RANKS + t) * width
            refs[RANKS][:, first : first + width] = pieces[t][:, p * width : (p + 1) * width]


def undeal(pieces, parts):
    rows, columns = pieces[0].shape
    return pl.pallas_call(
        functools.partial(undeal_kernel, parts),
        out_shape=jax.ShapeDtypeStruct((rows, columns * RANKS), F32),
    )(*pieces)


ROOM = 640
EXTRA = 8
SHORT = {}
for _name, _size in (
    ("gain1", 48),
    ("bias1", 48),
    ("gain2", 48),
    ("bias2", 48),
    ("b_in", 96),
    ("b_hid", 48),
    ("m", 48),
    ("p", 48),
    ("d0", 48),
    ("d1", 48),
    ("d2", 48),
    ("con", 16),
    ("pos", 16),
):
    _first = sum(_high - _low for _low, _high in SHORT.values())
    SHORT[_name] = (_first, _first + _size)
DEVICES = WINDOWS * RANKS
REL = HK // DEVICES


def pack_kernel(names, *refs):
    out_ref = refs[-1]
    out_ref[...] = jnp.zeros_like(out_ref)
    for name, ref in zip(names, refs):
        low, high = SHORT[name]
        out_ref[0:1, low:high] = ref[...].astype(F32)
    for b in range(BASIS):
        out_ref[1:2, b * REL : (b + 1) * REL] = refs[-2][b : b + 1, :].astype(F32)


def pack(rows, rel):
    return pl.pallas_call(
        functools.partial(pack_kernel, tuple(rows)),
        out_shape=jax.ShapeDtypeStruct((EXTRA, ROOM), F32),
    )(*(row[None] for row in rows.values()), rel)


WIDE = ("gain1", "bias1", "gain2", "bias2", "b_hid", "m", "p", "d0", "d1", "d2")


def unpack_kernel(table_ref, wide_ref, in_ref, con_ref, pos_ref, rel_ref):
    rank = lax.axis_index(SEQ)
    for d in range(DEVICES):
        line = table_ref[d][0:1]
        for number, name in enumerate(WIDE):
            low, high = SHORT[name]
            wide_ref[number : number + 1, d * 48 : (d + 1) * 48] = line[:, low:high]
    low, high = SHORT["b_in"]
    for w in range(WINDOWS):
        in_ref[0:1, w * 96 : (w + 1) * 96] = table_ref[RANKS * w + rank][0:1, low:high]
    here = DEVICES // RANKS
    for j in range(here):
        block = table_ref[here * rank + j]
        columns = slice(j * REL, (j + 1) * REL)
        for ref, name in ((con_ref, "con"), (pos_ref, "pos")):
            low, high = SHORT[name]
            ref[0:1, columns] = block[0:1, low:high]
        for b in range(BASIS):
            rel_ref[b : b + 1, columns] = block[1:2, b * REL : (b + 1) * REL]


def unpack(table):
    hq = HK // RANKS
    shapes = ((16, D), (1, FF // RANKS), (1, hq), (1, hq), (BASIS, hq))
    return pl.pallas_call(
        unpack_kernel, out_shape=[jax.ShapeDtypeStruct(shape, F32) for shape in shapes]
    )(table)


def pack_grads_kernel(names, *refs):
    rank = lax.axis_index(SEQ)
    wide, (in_ref, con_ref, pos_ref, rel_ref, out_ref) = refs[:-5], refs[-5:]
    out_ref[...] = jnp.zeros_like(out_ref)
    for d in range(DEVICES):
        for name, ref in zip(names, wide):
            low, high = SHORT[name]
            out_ref[d, 0:1, low:high] = ref[0:1, d * 48 : (d + 1) * 48]
    low, high = SHORT["b_in"]
    for w in range(WINDOWS):
        out_ref[RANKS * w + rank, 0:1, low:high] = in_ref[0:1, w * 96 : (w + 1) * 96]
    here = DEVICES // RANKS
    for j in range(here):
        columns = slice(j * REL, (j + 1) * REL)
        for ref, name in ((con_ref, "con"), (pos_ref, "pos")):
            low, high = SHORT[name]
            out_ref[here * rank + j, 0:1, low:high] = ref[0:1, columns]
        for b in range(BASIS):
            out_ref[here * rank + j, 1:2, b * REL : (b + 1) * REL] = rel_ref[
                b : b + 1, columns
            ]


def pack_grads(rows, in_row, con, pos, rel):
    return pl.pallas_call(
        functools.partial(pack_grads_kernel, tuple(rows)),
        out_shape=jax.ShapeDtypeStruct((DEVICES, EXTRA, ROOM), F32),
    )(*(row.reshape(1, -1) for row in rows.values()), in_row[None], con[None], pos[None], rel)


def finish_kernel(hq, hv, height, *refs):
    rank = lax.axis_index(SEQ)
    pieces, (q_ref, k_ref, v_ref, short_ref, rel_ref) = refs[:RANKS], refs[RANKS:]
    extra = jnp.zeros((EXTRA, ROOM), F32)
    for k in range(RANKS):
        block = pieces[k][...].astype(F32)
        t = rank ^ k
        weights = block[:height]
        narrow = pl.ds(pl.multiple_of(t * hq, 128), hq)
        q_ref[:, narrow] = weights[:, :hq]
        k_ref[:, narrow] = weights[:, hq : 2 * hq]
        v_ref[:, pl.ds(pl.multiple_of(t * hv, 128), hv)] = weights[:, 2 * hq :]
        extra = extra + block[height:]
    short_ref[...] = extra[0:1]
    for b in range(BASIS):
        rel_ref[b : b + 1, :] = extra[1:2, b * REL : (b + 1) * REL]


def finish(pieces, hq, hv):
    height = pieces[0].shape[0] - EXTRA
    shapes = ((height, HK), (height, HK), (height, HV), (1, ROOM), (BASIS, REL))
    return pl.pallas_call(
        functools.partial(finish_kernel, hq, hv, height),
        out_shape=[jax.ShapeDtypeStruct(shape, F32) for shape in shapes],
    )(*pieces)


def edges(rows, axis):
    count = lax.axis_size(axis)
    below, above = yield (
        lax.ppermute(rows[-1:], axis, [(i, i + 1) for i in range(count - 1)]),
        lax.ppermute(rows[:1], axis, [(i + 1, i) for i in range(count - 1)]),
    )
    return jnp.concatenate([below, rows, above], axis=0)


def win_all(block):
    got = yield [trade(block, WIN, 2 * k) for k in range(1, WINDOWS // 2)]
    column = place([block] + got, WIN, 2)
    beside = yield trade(column, WIN, 1)
    both = place([column, beside], WIN, 1, WINDOWS // 2)
    return both.reshape((WINDOWS,) + block.shape)


def z_sum(column, z):
    got = yield trade(jnp.stack([pick(column, z ^ 1), pick(column, z ^ 3)]), WIN, 2)
    last = yield trade(plus(pick(column, z ^ 2), got[1]), WIN, 4)
    return pick(column, z).astype(F32) + got[0].astype(F32) + last.astype(F32)


def win_sum(kept, sent, window):
    got = yield trade(sent, WIN, 1)
    total = yield from z_sum(plus(kept, got), window // 2)
    return total


def shared_sum(row):
    for axis, bits in ((WIN, 1), (WIN, 2), (WIN, 4), (SEQ, 1), (SEQ, 2)):
        got = yield trade(row, axis, bits)
        row = row + got
    return row


def split_kernel(axis, height, first_ref, second_ref, kept_ref, sent_ref):
    grads = weight_product(first_ref[...], second_ref[...]).astype(LOW)
    odd = lax.axis_index(axis) % 2
    for pair in range(kept_ref.shape[0]):
        low = 2 * pair * height
        even_rows = grads[low : low + height]
        odd_rows = grads[low + height : low + 2 * height]

        @pl.when(odd == 0)
        def _():
            kept_ref[pair] = even_rows
            sent_ref[pair] = odd_rows

        @pl.when(odd == 1)
        def _():
            kept_ref[pair] = odd_rows
            sent_ref[pair] = even_rows


def split_product(first_arg, second_arg, axis, height):
    depth, rows = first_arg.shape
    columns = second_arg.shape[1]
    width = 384 if rows % 384 == 0 else 640
    pairs = width // (2 * height)
    out = jax.ShapeDtypeStruct((rows // (2 * height), height, columns), LOW)
    out_spec = pl.BlockSpec((pairs, height, columns), lambda i: (i, 0, 0))
    return pl.pallas_call(
        functools.partial(split_kernel, axis, height),
        grid=(rows // width,),
        in_specs=[pl.BlockSpec((depth, width), lambda i: (0, i)), whole_spec(second_arg)],
        out_specs=[out_spec, out_spec],
        out_shape=[out, out],
        compiler_params=pltpu.CompilerParams(vmem_limit_bytes=32 * 2**20),
        cost_estimate=pl.CostEstimate(
            flops=2 * depth * rows * columns,
            transcendentals=0,
            bytes_accessed=2 * (depth * rows + depth * columns + rows * columns),
        ),
    )(first_arg, second_arg)


def core_sum(first_arg, second_arg):
    height = first_arg.shape[1] // DEVICES
    kept, sent = split_product(first_arg, second_arg, SEQ, height)
    got = yield trade(sent, SEQ, 1)
    return plus(kept, got).reshape((4, 2, 2) + kept.shape[1:])


def plus(first_arg, *others):
    total = first_arg.astype(F32)
    for other in others:
        total = total + other.astype(F32)
    return total.astype(LOW)


def z_chip_sum(grads, rank, window):
    z, y = window // 2, window % 2
    x = rank // 2
    height, columns = grads.shape[3:]
    total = yield from z_sum(grads.reshape(4, 4 * height, columns), z)
    total = total.astype(LOW).reshape(2, 2, height, columns)
    got = yield trade(pick(total, 1 - y), WIN, 1)
    both = plus(pick(total, y), got)
    got = yield trade(pick(both, 1 - x), SEQ, 2)
    return pick(both, x).astype(F32) + got.astype(F32)


def chip_sum(grads, rank, window, y_first):
    z, y = window // 2, window % 2
    x = rank // 2
    heights = [g.shape[3] for g in grads]

    def half(index):
        axis = 1 if y_first else 2
        cut = [lax.dynamic_index_in_dim(g, index, axis, keepdims=False) for g in grads]
        return cut[0] if len(cut) == 1 else jnp.concatenate(cut, axis=2)

    def quarter(both, index):
        return lax.dynamic_index_in_dim(both, index, 1, keepdims=False)

    first, second = (y, x) if y_first else (x, y)
    steps = ((WIN, 1), (SEQ, 2)) if y_first else ((SEQ, 2), (WIN, 1))
    got = yield trade(half(1 - first), *steps[0])
    both = plus(half(first), got)
    got = yield trade(quarter(both, 1 - second), *steps[1])
    total = yield from z_sum(plus(quarter(both, second), got), z)
    results, low = [], 0
    for height in heights:
        results.append(total[low : low + height])
        low += height
    return results


def split_body(
    inputs,
    skips,
    counts,
    ln1_gain,
    ln1_bias,
    w_query,
    w_key,
    w_value,
    w_rel,
    content_bias,
    position_bias,
    w_out,
    ln2_gain,
    ln2_bias,
    w_in,
    b_in,
    w_hid,
    b_hid,
    w_up,
    w_skip,
    m_bias,
    w_depth,
    w_point,
    p_bias,
    w_head,
    head_bias,
):
    window, rank = lax.axis_index(WIN), lax.axis_index(SEQ)
    seq_len = ROWS * RANKS
    hq, hv, ff = HK // RANKS, HV // RANKS, FF // RANKS

    packed = pack(
        {
            "gain1": ln1_gain,
            "bias1": ln1_bias,
            "gain2": ln2_gain,
            "bias2": ln2_bias,
            "b_in": b_in,
            "b_hid": b_hid,
            "m": m_bias,
            "p": p_bias,
            "d0": w_depth[0],
            "d1": w_depth[1],
            "d2": w_depth[2],
            "con": content_bias,
            "pos": position_bias,
        },
        w_rel,
    ).astype(LOW)
    qkv_local = jnp.stack(
        [
            jnp.concatenate(
                [
                    jnp.concatenate(
                        [
                            w_query[:, t * hq : (t + 1) * hq],
                            w_key[:, t * hq : (t + 1) * hq],
                            w_value[:, t * hv : (t + 1) * hv],
                        ],
                        axis=1,
                    ),
                    packed,
                ]
            )
            for t in range(RANKS)
        ]
    )
    qkv_flow = Flow(seq_swap(qkv_local, rank))
    four = lax.all_gather(jnp.concatenate([w_out, w_up, w_skip, w_point]), BOTH, axis=0)
    inputs_own, w_in, w_hid = advance((inputs.reshape(ROWS, D), w_in, w_hid), qkv_flow)
    qkv_flow = Flow(win_all(place(qkv_flow.result, SEQ).reshape(-1, ROOM)))
    inputs_flow = Flow(seq_all(inputs_own))
    dealt, w_hid, w_head = advance((deal(w_in, WINDOWS), w_hid, w_head), qkv_flow, inputs_flow)
    in_flow = Flow(seq_swap(dealt, rank))
    hid_flow = Flow(win_all(w_hid))
    head_full = lax.all_gather(w_head, BOTH, axis=0, tiled=True)
    advance((), qkv_flow, in_flow, inputs_flow)
    gathered = qkv_flow.result.reshape(DEVICES, -1, ROOM)
    height = gathered.shape[1] - EXTRA
    qkv_part = gathered[:, :height].reshape(D, ROOM)
    wide, in_bias, content, position, rel_part, qkv_part, inputs_all, in_rows = advance(
        (
            *unpack(gathered[:, height:].astype(F32)),
            qkv_part,
            inputs_flow.result,
            place(in_flow.result, SEQ).reshape(-1, ff),
        ),
        hid_flow,
    )
    in_flow = Flow(win_all(in_rows))
    row_of = {name: wide[number] for number, name in enumerate(WIDE)}
    depth_full = [row_of[name] for name in ("d0", "d1", "d2")]
    heads_here = hq // KEY
    same_head = (
        jnp.arange(hq)[:, None] // KEY == jnp.arange(heads_here * BASIS)[None, :] // BASIS
    )
    rel_square = jnp.where(same_head, jnp.tile(rel_part.T, (1, heads_here)), 0.0)
    gain_one, bias_one = row_of["gain1"], row_of["bias1"]
    gain_two, bias_two = row_of["gain2"], row_of["bias2"]

    normed = layer_norm(inputs_all.astype(F32), gain_one, bias_one).astype(LOW)
    projected = product(normed, qkv_part)
    query_raw = projected[:, :hq] * 0.125
    queries = (query_raw + content).astype(LOW)
    pos_in = query_raw + position
    pos_query = jnp.dot(pos_in, rel_square, precision=HIGH).astype(LOW)
    keys = projected[:, hq : 2 * hq].astype(LOW)
    values = projected[:, 2 * hq :].astype(LOW)
    offsets = wide_table(seq_len)
    mixed, norms = advance(
        mix(queries, keys, values, pos_query, offsets), in_flow, hid_flow
    )
    swap = Flow(seq_swap(mixed.reshape(RANKS, ROWS, hv), rank))
    norms = advance(norms, swap)
    attended = place(swap.result, SEQ, columns=True)
    r_out = w_out.shape[0]
    out_full = four[:, :r_out].reshape(HV, D)
    inputs_f = inputs_own.astype(F32)
    resid_one = inputs_f + product(attended, out_full)
    normed_flow = Flow(seq_all(layer_norm(resid_one, gain_two, bias_two).astype(LOW)))
    four = advance(four, normed_flow, in_flow)
    advance((), normed_flow)
    wholes, low = [], r_out
    for own in (w_up, w_skip, w_point):
        high = low + own.shape[0]
        wholes.append(four[:, low:high].reshape(-1, D))
        low = high
    up_full, skip_full, point_full = wholes
    normed_two = normed_flow.result
    in_part = in_flow.result.reshape(D, ff)
    hid_part = hid_flow.result.reshape(ff, D)
    pre_act = product(normed_two, in_part) + in_bias
    hidden = smooth_act(pre_act).astype(LOW)
    ff_flow = Flow(seq_sum(product(hidden, hid_part).astype(LOW), rank))
    skip_rows = advance(skips.reshape(2 * ROWS, CS), ff_flow)
    from_skips = product(skip_rows, skip_full) + row_of["m"]
    from_skips = advance(from_skips, ff_flow)
    lift_in = (resid_one + ff_flow.result + row_of["b_hid"]).astype(LOW)
    twice = (jnp.arange(2 * ROWS)[:, None] // 2 == jnp.arange(ROWS)[None, :]).astype(LOW)
    merged = product(product(twice, lift_in).astype(LOW), up_full) + from_skips
    merged_flow = Flow(edges(merged.astype(LOW), SEQ))
    merged = advance(merged, merged_flow)
    padded = merged_flow.result.astype(F32)
    depth_out = (
        depth_full[0] * padded[:-2] + depth_full[1] * padded[1:-1] + depth_full[2] * padded[2:]
    ).astype(LOW)
    output = merged + product(depth_out, point_full) + row_of["p"]
    head_rows = output.astype(LOW)
    logits = product(head_rows, head_full) + head_bias.astype(F32)
    rate_rows = jax.nn.softplus(logits)
    count_rows = counts.reshape(2 * ROWS, TRACKS).astype(F32)
    total_rate, total_count = lax.psum(
        (jnp.sum(rate_rows, axis=0), jnp.sum(count_rows, axis=0)), SEQ
    )
    log_total = jnp.log(total_rate)
    window_terms = jnp.sum(total_count * log_total) + 0.2 * jnp.sum(
        total_rate - total_count * log_total
    )
    local_loss = -jnp.sum(count_rows * jnp.log(rate_rows)) + jnp.where(
        rank == 0, window_terms, 0.0
    )
    grad_rate = -count_rows / rate_rows + (0.2 + 0.8 * (total_count / total_rate))
    grad_rows = (grad_rate * jax.nn.sigmoid(logits)).astype(LOW)
    head_bias_part = jnp.sum(grad_rows, axis=0, dtype=F32)
    shared_flow = Flow(shared_sum(jnp.concatenate([head_bias_part, local_loss[None]])))
    head_core = Flow(core_sum(head_rows, grad_rows))
    grad_out = input_product(grad_rows, head_full).astype(LOW)
    grad_depth = input_product(grad_out, point_full).astype(LOW)
    grad_out, grad_depth = advance((grad_out, grad_depth), head_core, shared_flow)
    depth_flow = Flow(edges(grad_depth, SEQ))
    grad_out, grad_depth = advance((grad_out, grad_depth), depth_flow, shared_flow)
    head_flow = Flow(z_chip_sum(head_core.result, rank, window))
    depth_pad = depth_flow.result
    merged_low = (
        grad_out.astype(F32)
        + depth_full[0] * depth_pad[2:]
        + depth_full[1] * depth_pad[1:-1]
        + depth_full[2] * depth_pad[:-2]
    ).astype(LOW)
    lift_grad = weight_product(twice, merged_low).astype(LOW)
    grad_two = input_product(lift_grad, up_full).astype(LOW)
    grad_two, merged_low, lift_grad = advance((grad_two, merged_low, lift_grad))
    two_flow = Flow(seq_all(grad_two))
    point_core = Flow(core_sum(depth_out, grad_out))
    skip_grad = input_product(merged_low, skip_full).reshape(1, 2 * ROWS, CS)
    depth_grad = jnp.stack(
        [
            jnp.sum(grad_depth * padded[:-2], axis=0),
            jnp.sum(grad_depth * padded[1:-1], axis=0),
            jnp.sum(grad_depth * padded[2:], axis=0),
        ]
    )
    skip_grad, merged_low, grad_two, depth_grad = advance(
        (skip_grad, merged_low, grad_two, depth_grad), two_flow, point_core, shared_flow
    )
    skip_core = Flow(core_sum(skip_rows, merged_low))
    up_core = Flow(core_sum(lift_in, lift_grad))
    pbias_grad = jnp.sum(grad_out, axis=0, dtype=F32)
    mbias_grad = jnp.sum(merged_low, axis=0, dtype=F32)
    hbias_grad = jnp.sum(grad_two, axis=0, dtype=F32)
    point_flow = Flow(chip_sum([point_core.result], rank, window, False))
    pbias_grad, mbias_grad, hbias_grad = advance(
        (pbias_grad, mbias_grad, hbias_grad), two_flow, skip_core, up_core, shared_flow
    )
    up_flow = Flow(chip_sum([up_core.result], rank, window, True))
    grad_two_all = two_flow.result
    grad_hidden = input_product(grad_two_all, hid_part).astype(LOW)
    _, pull_act = jax.vjp(smooth_act, pre_act)
    grad_pre = pull_act(grad_hidden.astype(F32))[0].astype(LOW)
    pre_flow = Flow(seq_sum(input_product(grad_pre, in_part).astype(LOW), rank))
    hid_parts = split_product(hidden, grad_two_all, WIN, ff // WINDOWS)
    in_parts = split_product(normed_two, grad_pre, WIN, D // WINDOWS)
    hid_parts, in_parts, grad_pre, skips_kept = advance(
        (hid_parts, in_parts, grad_pre, skip_core.result),
        pre_flow,
        point_flow,
        shared_flow,
    )
    hid_flow = Flow(win_sum(*hid_parts, window))
    ibias_part = jnp.sum(grad_pre, axis=0, dtype=F32)
    ibias_part, in_parts = advance(
        (ibias_part, in_parts), pre_flow, up_flow, point_flow, head_flow
    )
    _, pull_two = jax.vjp(layer_norm, resid_one, gain_two, bias_two)
    grad_resid, gain_two_grad, bias_two_grad = pull_two(pre_flow.result)
    grad_one = (grad_two.astype(F32) + grad_resid).astype(LOW)
    grad_att = input_product(grad_one, out_full).astype(LOW)
    att_flow = Flow(
        seq_swap(
            jnp.stack([grad_att[:, t * hv : (t + 1) * hv] for t in range(RANKS)]), rank
        )
    )
    grad_one, gain_two_grad, bias_two_grad, skips_kept, in_parts = advance(
        (grad_one, gain_two_grad, bias_two_grad, skips_kept, in_parts),
        att_flow,
        hid_flow,
    )
    in_flow = Flow(win_sum(*in_parts, window))
    out_core = Flow(core_sum(attended, grad_one))
    grad_att = place(att_flow.result, SEQ).reshape(seq_len, hv)
    query_low, pos_low, key_grad, value_grad, skips_kept = advance(
        (
            *mix_grad(queries, keys, values, pos_query, offsets, norms, grad_att),
            skips_kept,
        ),
        in_flow,
        out_core,
        up_flow,
    )
    rest_flow = Flow(chip_sum([skips_kept, out_core.result], rank, window, False))
    pos_f = pos_low.astype(F32)
    pos_in_grad = lax.dot_general(
        pos_f, rel_square, (((1,), (1,)), ((), ())), precision=HIGH
    )
    query_grad = (0.125 * (query_low.astype(F32) + pos_in_grad)).astype(LOW)
    qkv_out = jnp.concatenate([query_grad, key_grad, value_grad], axis=1)
    content_part = jnp.sum(query_low, axis=0, dtype=F32)
    rel_cross = lax.dot_general(pos_f, pos_in, (((0,), (0,)), ((), ())), precision=HIGH)
    rel_rows = jnp.sum(
        jnp.where(same_head.T, rel_cross, 0.0).reshape(heads_here, BASIS, hq), axis=0
    )
    position_part = jnp.sum(pos_in_grad, axis=0)
    partial = input_product(qkv_out, qkv_part).astype(LOW)
    centred = inputs_all.astype(F32)
    centred = centred - jnp.mean(centred, axis=-1, keepdims=True)
    scale = lax.rsqrt(jnp.mean(centred * centred, axis=-1, keepdims=True) + EPS)
    gain_one_grad = jnp.sum(partial * (centred * scale), axis=0)
    bias_one_grad = jnp.sum(partial, axis=0, dtype=F32)
    extra = pack_grads(
        {
            "gain1": gain_one_grad,
            "bias1": bias_one_grad,
            "gain2": gain_two_grad,
            "bias2": bias_two_grad,
            "b_hid": hbias_grad,
            "m": mbias_grad,
            "p": pbias_grad,
            "d0": depth_grad[0],
            "d1": depth_grad[1],
            "d2": depth_grad[2],
        },
        ibias_part,
        content_part,
        position_part,
        rel_rows,
    ).astype(LOW)
    qkv_kept, qkv_sent = split_product(normed, qkv_out, WIN, D // WINDOWS)
    y = window % 2
    extra = extra.reshape(WINDOWS // 2, 2, RANKS, EXTRA, ROOM)

    def with_extra(grads, index):
        grads = grads.reshape(WINDOWS // 2, RANKS, -1, ROOM)
        short = lax.dynamic_index_in_dim(extra, index, 1, keepdims=False)
        return jnp.concatenate([grads, short], axis=2).reshape(WINDOWS // 2, -1, ROOM)

    qkv_kept, qkv_sent = advance(
        (with_extra(qkv_kept, y), with_extra(qkv_sent, 1 - y)),
        in_flow,
        hid_flow,
        point_flow,
        head_flow,
    )
    qkv_flow = Flow(win_sum(qkv_kept, qkv_sent, window))
    one_flow = Flow(seq_sum(partial, rank))
    advance((), one_flow, in_flow, hid_flow, qkv_flow)
    in_back = in_flow.result.astype(LOW).reshape(RANKS, -1, ff)
    in_back = advance(in_back, one_flow, qkv_flow, up_flow, head_flow, rest_flow)
    in_back = Flow(seq_swap_two(in_back, rank))
    grad_normed = one_flow.result
    _, pull_one = jax.vjp(lambda rows: layer_norm(rows, gain_one, bias_one), inputs_f)
    (grad_norm_in,) = pull_one(grad_normed)
    grad_inputs = (grad_one.astype(F32) + grad_norm_in).reshape(1, ROWS, D)
    advance((), qkv_flow, in_back, rest_flow, head_flow, up_flow)
    qkv_flow = Flow(seq_swap(qkv_flow.result.astype(LOW).reshape(RANKS, -1, ROOM), rank))
    advance((), qkv_flow, in_back, rest_flow)
    advance((), rest_flow, point_flow)
    wq_grad, wk_grad, wv_grad, shorts, rel_grad = finish(qkv_flow.result, hq, hv)
    sums = {name: shorts[0, low:high] for name, (low, high) in SHORT.items()}
    in_grad = undeal(in_back.result, WINDOWS)
    (point_grad,), (up_grad,) = point_flow.result, up_flow.result
    skip_weight_grad, out_grad = rest_flow.result
    head_grad = head_flow.result
    hid_grad = hid_flow.result
    loss_total, head_bias_grad = shared_flow.result[-1], shared_flow.result[:-1]
    loss_mean = loss_total / (WINDOWS * 2 * seq_len * TRACKS)
    return (
        loss_mean,
        head_rows.reshape(1, 2 * ROWS, D),
        grad_inputs,
        skip_grad,
        sums["gain1"],
        sums["bias1"],
        wq_grad,
        wk_grad,
        wv_grad,
        rel_grad,
        sums["con"],
        sums["pos"],
        out_grad,
        sums["gain2"],
        sums["bias2"],
        in_grad,
        sums["b_in"],
        hid_grad,
        sums["b_hid"],
        up_grad,
        skip_weight_grad,
        sums["m"],
        jnp.stack([sums["d0"], sums["d1"], sums["d2"]]),
        point_grad,
        sums["p"],
        head_grad,
        head_bias_grad,
    )


def general_body(
    inputs,
    skips,
    counts,
    ln1_gain,
    ln1_bias,
    w_query,
    w_key,
    w_value,
    w_rel,
    content_bias,
    position_bias,
    w_out,
    ln2_gain,
    ln2_bias,
    w_in,
    b_in,
    w_hid,
    b_hid,
    w_up,
    w_skip,
    m_bias,
    w_depth,
    w_point,
    p_bias,
    w_head,
    head_bias,
):
    seq_count = lax.axis_size(SEQ)
    seq_len = TOK_SEQ * seq_count
    first_pos = lax.axis_index(SEQ) * TOK_SEQ
    row_count = SEQS_DEV * TOK_SEQ
    blk_len = 512
    blk_count = seq_len // blk_len
    blk_steps = jnp.arange(blk_count, dtype=jnp.int32)
    mixer_full = (
        lax.all_gather(ln1_gain, BOTH, axis=0, tiled=True),
        lax.all_gather(ln1_bias, BOTH, axis=0, tiled=True),
        lax.all_gather(w_query, BOTH, axis=0, tiled=True),
        lax.all_gather(w_key, BOTH, axis=0, tiled=True),
        lax.all_gather(w_value, BOTH, axis=0, tiled=True),
        lax.all_gather(w_rel, BOTH, axis=1, tiled=True),
        lax.all_gather(content_bias, BOTH, axis=0, tiled=True),
        lax.all_gather(position_bias, BOTH, axis=0, tiled=True),
        lax.all_gather(w_out, BOTH, axis=0, tiled=True),
    )
    tail_full = (
        lax.all_gather(ln2_gain, BOTH, axis=0, tiled=True),
        lax.all_gather(ln2_bias, BOTH, axis=0, tiled=True),
        lax.all_gather(w_in, BOTH, axis=0, tiled=True),
        lax.all_gather(b_in, BOTH, axis=0, tiled=True),
        lax.all_gather(w_hid, BOTH, axis=0, tiled=True),
        lax.all_gather(b_hid, BOTH, axis=0, tiled=True),
        lax.all_gather(w_up, BOTH, axis=0, tiled=True),
        lax.all_gather(w_skip, BOTH, axis=0, tiled=True),
        lax.all_gather(m_bias, BOTH, axis=0, tiled=True),
        lax.all_gather(w_depth, BOTH, axis=1, tiled=True),
        lax.all_gather(w_point, BOTH, axis=0, tiled=True),
        lax.all_gather(p_bias, BOTH, axis=0, tiled=True),
        lax.all_gather(w_head, BOTH, axis=0, tiled=True),
    )
    gain_one = mixer_full[0].astype(jnp.float32)
    bias_one = mixer_full[1].astype(jnp.float32)
    query_full = mixer_full[2]
    key_full = mixer_full[3]
    value_full = mixer_full[4]
    rel_full = mixer_full[5].astype(jnp.float32).reshape(BASIS, HEADS, KEY)
    content_full = mixer_full[6].astype(jnp.float32)
    position_full = mixer_full[7].astype(jnp.float32)
    out_full = mixer_full[8]
    gain_two = tail_full[0].astype(jnp.float32)
    bias_two = tail_full[1].astype(jnp.float32)
    in_full = tail_full[2]
    in_bias = tail_full[3].astype(jnp.float32)
    hid_full = tail_full[4]
    hid_bias = tail_full[5].astype(jnp.float32)
    up_full = tail_full[6]
    skip_full = tail_full[7]
    merge_bias = tail_full[8].astype(jnp.float32)
    depth_full = tail_full[9].astype(jnp.float32)
    point_full = tail_full[10]
    point_bias = tail_full[11].astype(jnp.float32)
    head_full = tail_full[12]
    inputs_f = inputs.astype(jnp.float32).reshape(row_count, D)
    normed = layer_norm(inputs_f, gain_one, bias_one).astype(jnp.bfloat16)
    query_raw = product(normed, query_full) * 0.125
    queries = (query_raw + content_full).astype(jnp.bfloat16).reshape(SEQS_DEV, TOK_SEQ, HEADS, KEY)
    pos_in = (query_raw + position_full).reshape(row_count, HEADS, KEY)
    pos_query = (
        jnp.einsum("lhk,bhk->lhb", pos_in, rel_full, precision=HIGH)
        .astype(jnp.bfloat16)
        .reshape(SEQS_DEV, TOK_SEQ, HEADS, BASIS)
    )
    key_rows = product(normed, key_full).astype(jnp.bfloat16).reshape(SEQS_DEV, TOK_SEQ, HK)
    values = product(normed, value_full).astype(jnp.bfloat16).reshape(SEQS_DEV, TOK_SEQ, HV)
    keys_all, values_all = (
        lax.all_gather(key_rows, SEQ, axis=1, tiled=True),
        lax.all_gather(values, SEQ, axis=1, tiled=True),
    )

    def key_block(whole_rows, blk_index):
        return lax.dynamic_slice_in_dim(whole_rows, blk_index * blk_len, blk_len, 1)

    def value_block(blk_index):
        return key_block(values_all, blk_index).reshape(SEQS_DEV, blk_len, HEADS, VAL)

    def scores_at(blk_index):
        return score_block(
            queries,
            pos_query,
            key_block(keys_all, blk_index),
            first_pos,
            blk_index * blk_len,
            seq_len,
        )

    def max_step(state_pair, blk_index):
        row_max, row_sum = state_pair
        scores, basis_grid = scores_at(blk_index)
        new_max = jnp.maximum(row_max, jnp.max(scores, axis=-1))
        row_sum = row_sum * jnp.exp(row_max - new_max) + jnp.sum(
            jnp.exp(scores - new_max[..., None]), axis=-1
        )
        return ((new_max, row_sum), None)

    start_max = jnp.full((SEQS_DEV, HEADS, TOK_SEQ), -jnp.inf, jnp.float32)
    (row_max, row_sum), _ = lax.scan(max_step, (start_max, jnp.zeros_like(start_max)), blk_steps)
    log_norm = row_max + jnp.log(row_sum)

    def mix_step(mixed_sum, blk_index):
        scores, basis_grid = scores_at(blk_index)
        weights = jnp.exp(scores - log_norm[..., None]).astype(jnp.bfloat16)
        mixed_sum = mixed_sum + jnp.einsum(
            "shnc,schv->snhv", weights, value_block(blk_index), preferred_element_type=jnp.float32
        )
        return (mixed_sum, None)

    mixed_sum, _ = lax.scan(
        mix_step, jnp.zeros((SEQS_DEV, TOK_SEQ, HEADS, VAL), jnp.float32), blk_steps
    )
    attended = mixed_sum.reshape(row_count, HV).astype(jnp.bfloat16)
    resid_one = inputs_f + product(attended, out_full)
    normed_two = layer_norm(resid_one, gain_two, bias_two).astype(jnp.bfloat16)
    pre_act = product(normed_two, in_full) + in_bias
    hidden = smooth_act(pre_act).astype(jnp.bfloat16)
    lift_in = (resid_one + product(hidden, hid_full) + hid_bias).astype(jnp.bfloat16)
    lifted = product(lift_in, up_full).reshape(SEQS_DEV, TOK_SEQ, D)
    skip_rows = skips.reshape(2 * row_count, CS)
    merged = (
        jnp.repeat(lifted, 2, axis=1)
        + product(skip_rows, skip_full).reshape(SEQS_DEV, 2 * TOK_SEQ, D)
        + merge_bias
    )
    padded = with_halo(merged.astype(jnp.bfloat16), ((SEQ, 1),), 1).astype(merged.dtype)
    depth_out = (
        depth_full[0] * padded[:, :-2]
        + depth_full[1] * padded[:, 1:-1]
        + depth_full[2] * padded[:, 2:]
    ).astype(jnp.bfloat16)
    output = (
        merged
        + product(depth_out.reshape(2 * row_count, D), point_full).reshape(SEQS_DEV, 2 * TOK_SEQ, D)
        + point_bias
    )
    head_in = output.astype(jnp.bfloat16)
    head_rows = head_in.reshape(2 * row_count, D)
    logits = (product(head_rows, head_full) + head_bias.astype(jnp.float32)).reshape(
        SEQS_DEV, 2 * TOK_SEQ, TRACKS
    )
    rate_rows = jax.nn.softplus(logits)
    count_rows = counts.astype(jnp.float32)
    part_rate = jnp.sum(rate_rows, axis=1)
    part_count = jnp.sum(count_rows, axis=1)
    total_rate, total_count = lax.psum((part_rate, part_count), SEQ)
    log_total = jnp.log(total_rate)
    window_terms = jnp.sum(total_count * log_total) + 0.2 * jnp.sum(
        total_rate - total_count * log_total
    )
    local_loss = -jnp.sum(count_rows * jnp.log(rate_rows)) + jnp.where(
        lax.axis_index(SEQ) == 0, window_terms, 0.0
    )
    count_ratio = total_count / total_rate
    grad_rate = -count_rows / rate_rows + (0.2 + 0.8 * count_ratio)[:, None, :]
    grad_logit = (grad_rate * jax.nn.sigmoid(logits)).astype(jnp.bfloat16)
    bias_part = jnp.sum(grad_logit, axis=(0, 1), dtype=jnp.float32)
    loss_total, head_bias_grad = lax.psum((local_loss, bias_part), BOTH)
    loss_mean = loss_total / (SEQS_DEV * lax.axis_size(WIN) * 2 * seq_len * TRACKS)
    grad_rows = grad_logit.reshape(2 * row_count, TRACKS)
    head_grad = weight_product(head_rows, grad_rows)
    grad_out = input_product(grad_rows, head_full).astype(jnp.bfloat16)
    point_grad = weight_product(depth_out.reshape(2 * row_count, D), grad_out)
    pbias_grad = jnp.sum(grad_out, axis=0, dtype=jnp.float32)
    grad_depth = (
        input_product(grad_out, point_full).astype(jnp.bfloat16).reshape(SEQS_DEV, 2 * TOK_SEQ, D)
    )
    depth_grad = jnp.stack(
        [
            jnp.sum(grad_depth * padded[:, :-2], axis=(0, 1)),
            jnp.sum(grad_depth * padded[:, 1:-1], axis=(0, 1)),
            jnp.sum(grad_depth * padded[:, 2:], axis=(0, 1)),
        ]
    )
    depth_pad = with_halo(grad_depth, ((SEQ, 1),), 1)
    grad_merged = (
        grad_out.reshape(SEQS_DEV, 2 * TOK_SEQ, D).astype(jnp.float32)
        + depth_full[0] * depth_pad[:, 2:]
        + depth_full[1] * depth_pad[:, 1:-1]
        + depth_full[2] * depth_pad[:, :-2]
    )
    merged_low = grad_merged.astype(jnp.bfloat16)
    merged_rows = merged_low.reshape(2 * row_count, D)
    skip_weight_grad = weight_product(skip_rows, merged_rows)
    skip_grad = input_product(merged_rows, skip_full).reshape(SEQS_DEV, 2 * TOK_SEQ, CS)
    mbias_grad = jnp.sum(merged_rows, axis=0, dtype=jnp.float32)
    lift_grad = (
        jnp.sum(merged_low.reshape(SEQS_DEV, TOK_SEQ, 2, D), axis=2, dtype=jnp.float32)
        .reshape(row_count, D)
        .astype(jnp.bfloat16)
    )
    up_grad = weight_product(lift_in, lift_grad)
    grad_two = input_product(lift_grad, up_full).astype(jnp.bfloat16)
    hid_grad = weight_product(hidden, grad_two)
    hbias_grad = jnp.sum(grad_two, axis=0, dtype=jnp.float32)
    grad_hidden = input_product(grad_two, hid_full).astype(jnp.bfloat16)
    _, pull_act = jax.vjp(smooth_act, pre_act)
    grad_pre = pull_act(grad_hidden.astype(jnp.float32))[0].astype(jnp.bfloat16)
    in_grad = weight_product(normed_two, grad_pre)
    ibias_grad = jnp.sum(grad_pre, axis=0, dtype=jnp.float32)
    _, pull_two = jax.vjp(layer_norm, resid_one, gain_two, bias_two)
    grad_resid, gain_two_grad, bias_two_grad = pull_two(input_product(grad_pre, in_full))
    grad_one = (grad_two.astype(jnp.float32) + grad_resid).astype(jnp.bfloat16)
    out_grad = weight_product(attended, grad_one)
    grad_att = (
        input_product(grad_one, out_full)
        .astype(jnp.bfloat16)
        .reshape(SEQS_DEV, TOK_SEQ, HEADS, VAL)
    )

    def grad_parts(blk_index):
        key_blk = key_block(keys_all, blk_index)
        scores, basis_grid = score_block(
            queries, pos_query, key_blk, first_pos, blk_index * blk_len, seq_len
        )
        soft_probs = jnp.exp(scores - log_norm[..., None])
        prob_grad = jnp.einsum(
            "snhv,schv->shnc", grad_att, value_block(blk_index), preferred_element_type=jnp.float32
        )
        return (key_blk, basis_grid, soft_probs, prob_grad)

    def delta_step(delta_sum, blk_index):
        key_blk, basis_grid, soft_probs, prob_grad = grad_parts(blk_index)
        return (delta_sum + jnp.sum(soft_probs * prob_grad, axis=-1), None)

    row_delta, _ = lax.scan(
        delta_step, jnp.zeros((SEQS_DEV, HEADS, TOK_SEQ), jnp.float32), blk_steps
    )

    def query_terms(state_pair, blk_index):
        key_blk, basis_grid, soft_probs, prob_grad = grad_parts(blk_index)
        score_grad = (soft_probs * (prob_grad - row_delta[..., None])).astype(jnp.bfloat16)
        key_heads = key_blk.reshape(SEQS_DEV, blk_len, HEADS, KEY)
        query_acc = state_pair[0] + jnp.einsum(
            "shnc,schk->snhk", score_grad, key_heads, preferred_element_type=jnp.float32
        )
        pos_acc = state_pair[1] + jnp.einsum(
            "shnc,ncb->snhb", score_grad, basis_grid, preferred_element_type=jnp.float32
        )
        return ((query_acc, pos_acc), score_grad, soft_probs)

    query_zero = jnp.zeros((SEQS_DEV, TOK_SEQ, HEADS, KEY), jnp.float32)
    pos_zero = jnp.zeros((SEQS_DEV, TOK_SEQ, HEADS, BASIS), jnp.float32)

    def sum_step(state_four, blk_index):
        pair_next, score_grad, soft_probs = query_terms((state_four[0], state_four[1]), blk_index)
        key_part = jnp.einsum(
            "shnc,snhk->schk", score_grad, queries, preferred_element_type=jnp.float32
        ).reshape(SEQS_DEV, blk_len, HK)
        value_part = jnp.einsum(
            "shnc,snhv->schv",
            soft_probs.astype(jnp.bfloat16),
            grad_att,
            preferred_element_type=jnp.float32,
        ).reshape(SEQS_DEV, blk_len, HV)
        key_acc = lax.dynamic_update_slice_in_dim(state_four[2], key_part, blk_index * blk_len, 1)
        value_acc = lax.dynamic_update_slice_in_dim(
            state_four[3], value_part, blk_index * blk_len, 1
        )
        return ((pair_next[0], pair_next[1], key_acc, value_acc), None)

    start_four = (
        query_zero,
        pos_zero,
        jnp.zeros((SEQS_DEV, seq_len, HK), jnp.float32),
        jnp.zeros((SEQS_DEV, seq_len, HV), jnp.float32),
    )
    (query_acc, pos_acc, key_terms_all, value_terms_all), _ = lax.scan(
        sum_step, start_four, blk_steps
    )
    key_sum, value_sum = (
        lax.psum_scatter(
            key_terms_all.astype(jnp.bfloat16), SEQ, scatter_dimension=1, tiled=True
        ).astype(jnp.float32),
        lax.psum_scatter(
            value_terms_all.astype(jnp.bfloat16), SEQ, scatter_dimension=1, tiled=True
        ).astype(jnp.float32),
    )
    key_grad = key_sum.reshape(row_count, HK).astype(jnp.bfloat16)
    value_grad = value_sum.reshape(row_count, HV).astype(jnp.bfloat16)
    query_low = query_acc.astype(jnp.bfloat16).reshape(row_count, HK)
    content_grad = jnp.sum(query_low, axis=0, dtype=jnp.float32)
    pos_low = pos_acc.astype(jnp.bfloat16).reshape(row_count, HEADS, BASIS).astype(jnp.float32)
    pos_in_grad = jnp.einsum("lhb,bhk->lhk", pos_low, rel_full, precision=HIGH)
    rel_grad = jnp.einsum("lhb,lhk->bhk", pos_low, pos_in, precision=HIGH).reshape(BASIS, HK)
    position_grad = jnp.sum(pos_in_grad, axis=0).reshape(HK)
    query_grad = (
        0.125 * (query_low.astype(jnp.float32) + pos_in_grad.reshape(row_count, HK))
    ).astype(jnp.bfloat16)
    wq_grad = weight_product(normed, query_grad)
    wk_grad = weight_product(normed, key_grad)
    wv_grad = weight_product(normed, value_grad)
    grad_normed = (
        input_product(query_grad, query_full)
        + input_product(key_grad, key_full)
        + input_product(value_grad, value_full)
    )
    _, pull_one = jax.vjp(layer_norm, inputs_f, gain_one, bias_one)
    grad_norm_in, gain_one_grad, bias_one_grad = pull_one(grad_normed)
    grad_inputs = (grad_one.astype(jnp.float32) + grad_norm_in).reshape(SEQS_DEV, TOK_SEQ, D)
    mixer_grads = (
        lax.psum_scatter(gain_one_grad, BOTH, scatter_dimension=0, tiled=True),
        lax.psum_scatter(bias_one_grad, BOTH, scatter_dimension=0, tiled=True),
        lax.psum_scatter(wq_grad, BOTH, scatter_dimension=0, tiled=True),
        lax.psum_scatter(wk_grad, BOTH, scatter_dimension=0, tiled=True),
        lax.psum_scatter(wv_grad, BOTH, scatter_dimension=0, tiled=True),
        lax.psum_scatter(rel_grad, BOTH, scatter_dimension=1, tiled=True),
        lax.psum_scatter(content_grad, BOTH, scatter_dimension=0, tiled=True),
        lax.psum_scatter(position_grad, BOTH, scatter_dimension=0, tiled=True),
        lax.psum_scatter(out_grad, BOTH, scatter_dimension=0, tiled=True),
    )
    tail_grads = (
        lax.psum_scatter(gain_two_grad, BOTH, scatter_dimension=0, tiled=True),
        lax.psum_scatter(bias_two_grad, BOTH, scatter_dimension=0, tiled=True),
        lax.psum_scatter(in_grad, BOTH, scatter_dimension=0, tiled=True),
        lax.psum_scatter(ibias_grad, BOTH, scatter_dimension=0, tiled=True),
        lax.psum_scatter(hid_grad, BOTH, scatter_dimension=0, tiled=True),
        lax.psum_scatter(hbias_grad, BOTH, scatter_dimension=0, tiled=True),
        lax.psum_scatter(up_grad, BOTH, scatter_dimension=0, tiled=True),
        lax.psum_scatter(skip_weight_grad, BOTH, scatter_dimension=0, tiled=True),
        lax.psum_scatter(mbias_grad, BOTH, scatter_dimension=0, tiled=True),
        lax.psum_scatter(depth_grad, BOTH, scatter_dimension=1, tiled=True),
        lax.psum_scatter(point_grad, BOTH, scatter_dimension=0, tiled=True),
        lax.psum_scatter(pbias_grad, BOTH, scatter_dimension=0, tiled=True),
        lax.psum_scatter(head_grad, BOTH, scatter_dimension=0, tiled=True),
    )
    return (
        (loss_mean, head_in, grad_inputs, skip_grad)
        + tuple(mixer_grads)
        + tuple(tail_grads)
        + (head_bias_grad,)
    )


SPLIT, ROWED, TILED = P(BOTH), P(BOTH, None), P(WIN, SEQ, None)


def solution(mesh):
    paired = mesh.shape[WIN] == 8 and mesh.shape[SEQ] == 4
    return jax.shard_map(
        split_body if paired else general_body,
        mesh=mesh,
        in_specs=(
            TILED,
            TILED,
            TILED,
            SPLIT,
            SPLIT,
            ROWED,
            ROWED,
            ROWED,
            P(None, BOTH),
            SPLIT,
            SPLIT,
            ROWED,
            SPLIT,
            SPLIT,
            ROWED,
            SPLIT,
            ROWED,
            SPLIT,
            ROWED,
            ROWED,
            SPLIT,
            P(None, BOTH),
            ROWED,
            SPLIT,
            ROWED,
            P(),
        ),
        out_specs=(
            P(),
            TILED,
            TILED,
            TILED,
            SPLIT,
            SPLIT,
            ROWED,
            ROWED,
            ROWED,
            P(None, BOTH),
            SPLIT,
            SPLIT,
            ROWED,
            SPLIT,
            SPLIT,
            ROWED,
            SPLIT,
            ROWED,
            SPLIT,
            ROWED,
            ROWED,
            SPLIT,
            P(None, BOTH),
            ROWED,
            SPLIT,
            ROWED,
            P(),
        ),
        check_vma=False,
    )
```
